32 devices in a mesh: slab: 8 (over z, y), sub: 4 (over x, core).
Axes of the slice: x: 2, y: 2, z: 4, core: 2. Of those that a mesh axis runs over, the one named last changes fastest.
Arguments:
- velocity: float32 [16384, 3, 128], P(('slab', 'sub')), may hold values from -6 to 6
- weight: float32 [16384, 128], P(('slab', 'sub')), may hold values from 0.2 to 2
- offset: int32 [16384, 128], P(('slab', 'sub')), may hold values from 0 to 127
- owner: int32 [16384, 1], P(('slab', 'sub')), may hold values from 0 to 31; in each aligned block of 512 rows (0 to 511, 512 to 1023, ...) at most 32 rows name the same one
- brick: int32 [16384, 1], P(('slab', 'sub')), may hold values from 0 to 4095
- flags: int32 [64, 256, 1024], P('slab', 'sub'), may hold values from 0 to 2, as said below
Outputs:
- updated: float32 [16384, 3, 128], P(('slab', 'sub'))
- pressure: float32 [64, 256, 1024], P('slab', 'sub')
- solved_face_velocity: float32 [3, 64, 256, 1024], P(None, 'slab', 'sub')
The draws below stay inside these ranges and needn't reach their ends.
Inputs may be any that keep to these rules, and one draw needn't show every extreme that they name: Among the blocks of one device, at most 32 name the same owner. `flags`: 0 air, 1 liquid, 2 solid.
All inputs are finite; a program needn't handle non-finite values.
Results may differ from the reference program's by a relative error of at most 0.000075.
Values sent between devices are 32-bit elements; how exact they have to be, the bound alone decides.
A program may use at most 128 MiB of HBM per device.

```python
import math
import jax
import jax.numpy as jnp
import numpy as np
from jax import lax

PB = 128
BC = 128
ITERS = 3
CX = 8
CY = 64
NZ = 1024
BLK_DEV = 512
NX = 64
NY = 256
BLOCKS = 16384
BRICKS_DEV = 4096
CAP = 32
N_SLAB = 8
N_SUB = 4
DEVICES = 32


def draw_flags(key, part):
    level = jax.random.randint(jax.random.fold_in(key, 7), (NX, NY, NZ), 0, 10)
    return jnp.where(level < 6, 1, jnp.where(level < 9, 0, 2)).astype(jnp.int32)


def place_ends(drawn, stream_key, low, top_value):
    shape = drawn.shape
    spot = [jax.random.randint(jax.random.fold_in(stream_key, axis), (), 0, shape[axis]) for axis in range(len(shape))]
    drawn = drawn.at[tuple(spot)].set(low)
    longest = shape.index(max(shape))
    spot[longest] = (spot[longest] + 1) % shape[longest]
    return drawn.at[tuple(spot)].set(top_value)


def block_scale(rng, dims, cuts, smallest, high):
    loudness, own = 1.0, jax.random.fold_in(rng, 6)
    for dim, blocks in cuts:
        heights = jnp.exp(jax.random.uniform(jax.random.fold_in(own, dim), (blocks,), jnp.float32, smallest / len(cuts), high / len(cuts)))
        loudness = loudness * jnp.repeat(heights, dims[dim] // blocks).reshape([-1 if axis == dim else 1 for axis in range(len(dims))])
    return loudness


def routed_block(own_key, own, number, rows, count, top, reach, lean):
    order = jax.random.permutation(own_key, count)
    heavy_load, usual = shares(count, rows * top, reach, lean, True), shares(count, rows * top, reach, lean, False)
    places = jnp.arange(count)

    def named(sizes, offset_by):
        used = int((sizes > 0).sum())
        fixed = max(1, used // 4)
        passed = fixed + (places - fixed + offset_by * (used - fixed)) % max(1, count - fixed)
        return jnp.zeros((count,), jnp.int32).at[order[jnp.where(places < fixed, places, passed)]].set(jnp.asarray(sizes, jnp.int32))

    sizes = jnp.where(number % 4 == 0, named(heavy_load, number // 4), named(usual, number - number // 4 - 1))
    mixed = jax.random.permutation(jax.random.fold_in(own, 3), count)
    donor, taker = mixed[0:count // 2 * 2:2], mixed[1:count // 2 * 2:2]
    slack = jnp.minimum(sizes[donor] - 1, reach - sizes[taker]) // 2
    slack = jnp.where((donor == order[0]) | (taker == order[0]) | (sizes[taker] == 0), 0, jnp.maximum(slack, 0))
    passed = jax.random.randint(jax.random.fold_in(own, 4), (count // 2,), 0, 1 << 20) % (slack + 1)
    sizes = sizes.at[donor].add(-passed).at[taker].add(passed)
    labels = jnp.searchsorted(jnp.cumsum(sizes), jnp.arange(rows * top), side="right").astype(jnp.int32)
    listing = labels.reshape(top, rows).T
    listing = listing[jax.random.permutation(jax.random.fold_in(own, 1), rows)]
    offset_by = jax.random.randint(jax.random.fold_in(own, 2), (rows, 1), 0, top)
    return jnp.take_along_axis(listing, (jnp.arange(top)[None, :] + offset_by) % top, axis=1)


def shares(number_of, total, limit, lean, full):
    weights = [(1 << 20) // math.isqrt(grade ** lean) + 1 for grade in range(1, number_of + 1)]
    largest = limit if full else min(limit, max(-(-total // number_of), total * weights[0] // sum(weights)))
    least = 1 if total - largest >= number_of - 1 else 0
    given, rest = [largest] + [least] * (number_of - 1), total - largest - least * (number_of - 1)
    while rest > 0:
        free = [i for i in range(1, number_of) if given[i] < largest] or [i for i in range(1, number_of) if given[i] < limit]
        whole, left = sum([weights[i] for i in free]), rest
        for i in free:
            addition = min(limit - given[i], max(1, left * weights[i] // whole), rest)
            given[i] = given[i] + addition
            rest = rest - addition
    return np.array(given)


def bell_draw(own_key, dims, scale, limit, cuts=(), held_as=jnp.bfloat16):
    drawn = scale * jax.random.normal(own_key, dims, jnp.float32)
    if cuts:
        drawn = drawn * block_scale(own_key, dims, cuts, -0.22, 0.18)
    return jnp.clip(drawn, -limit, limit).astype(held_as)


def setup_inputs(seed: int = 0) -> dict:
    streams_of = jax.random.split(jax.random.key(seed), 7)
    velocity = bell_draw(streams_of[0], (BLOCKS, 3, PB), 1.0, 6.0, ((0, 32),), jnp.float32)
    weight = jnp.clip(jnp.exp(math.log(2.0) - 2.3025851 * jax.random.uniform(streams_of[1], (BLOCKS, PB), jnp.float32) ** block_scale(streams_of[1], (BLOCKS, PB), ((0, 32),), -0.2, 0.2)), 0.2, 2.0)
    offset = place_ends(jax.random.randint(streams_of[2], (BLOCKS, PB), 0, BC), jax.random.fold_in(streams_of[2], 1), 0, BC - 1).astype(jnp.int32)
    owner_keys = jax.random.split(jax.random.fold_in(streams_of[3], 1), BLOCKS // BLK_DEV)
    owner_turns = jax.random.permutation(jax.random.fold_in(streams_of[3], 3), BLOCKS // BLK_DEV)
    owner = jax.vmap(lambda own, number: routed_block(jax.random.fold_in(streams_of[3], 2), own, number, BLK_DEV, DEVICES, 1, CAP, 2))(owner_keys, owner_turns).reshape((BLOCKS, 1))
    brick = place_ends(jax.random.randint(streams_of[4], (BLOCKS, 1), 0, BRICKS_DEV), jax.random.fold_in(streams_of[4], 1), 0, BRICKS_DEV - 1).astype(jnp.int32)
    flags = draw_flags(jax.random.fold_in(streams_of[6], 71), 0)
    return {"velocity": velocity, "weight": weight, "offset": offset, "owner": owner, "brick": brick, "flags": flags}


step_size = 0.15


def following(field, axis):
    edge = jnp.zeros_like(lax.slice_in_dim(field, 0, 1, axis=axis))
    return jnp.concatenate([lax.slice_in_dim(field, 1, field.shape[axis], axis=axis), edge], axis)


def preceding(field, axis):
    edge = jnp.zeros_like(lax.slice_in_dim(field, 0, 1, axis=axis))
    return jnp.concatenate([edge, lax.slice_in_dim(field, 0, field.shape[axis] - 1, axis=axis)], axis)


def reference(velocity, weight, offset, owner, brick, flags):
    target = owner[:, 0].astype(jnp.int32) * BRICKS_DEV + brick[:, 0].astype(jnp.int32)
    cell_index = (target[:, None] * BC + offset.astype(jnp.int32)).reshape(-1)
    loaded = jnp.concatenate([velocity * weight[:, None, :], weight[:, None, :]], 1)
    loaded = jnp.transpose(loaded, (0, 2, 1)).reshape(-1, 4)
    totals = jax.ops.segment_sum(loaded, cell_index, num_segments=DEVICES * BRICKS_DEV * BC)
    totals = totals.reshape(N_SLAB, N_SUB, CX, CY, NZ, 4).transpose(5, 0, 2, 1, 3, 4).reshape(4, NX, NY, NZ)
    metric = totals[3] + 1.0
    guess = totals[:3] / metric
    open_cell = (flags != 2).astype(jnp.float32)
    liquid = (flags == 1).astype(jnp.float32)
    faces_open = jnp.stack([open_cell * following(open_cell, axis) for axis in range(3)])
    solved_face_velocity = faces_open * guess
    pressure = jnp.zeros_like(metric)
    for sweep in range(ITERS):
        spread = solved_face_velocity[0] - preceding(solved_face_velocity[0], 0)
        spread = spread + (solved_face_velocity[1] - preceding(solved_face_velocity[1], 1))
        spread = spread + (solved_face_velocity[2] - preceding(solved_face_velocity[2], 2))
        pressure = liquid * jnp.maximum(pressure - step_size * spread, 0.0)
        push = jnp.stack([pressure - following(pressure, axis) for axis in range(3)])
        solved_face_velocity = faces_open * (guess + push / metric)
    change = solved_face_velocity - guess
    flat = change.reshape(3, N_SLAB, CX, N_SUB, CY, NZ).transpose(1, 3, 2, 4, 5, 0).reshape(-1, 3)
    picked = flat[cell_index].reshape(BLOCKS, PB, 3).transpose(0, 2, 1)
    return velocity + picked, pressure, solved_face_velocity
```

```python
import functools

import jax
import jax.numpy as jnp
from jax import lax
from jax.experimental import pallas as pl
from jax.experimental.pallas import tpu as pltpu
from jax.sharding import PartitionSpec as P

LANES = 128
SUB = 8
ITERS = 3

step_size = 0.15
MESH = pl.DeviceIdType.MESH
F32 = jnp.float32
I32 = jnp.int32
VMEM_LIMIT = 60 * 1024 * 1024


def vmem():
    return pl.BlockSpec(memory_space=pltpu.VMEM)


def smem():
    return pl.BlockSpec(memory_space=pltpu.SMEM)


def anywhere():
    return pl.BlockSpec(memory_space=pl.ANY)


def struct(shape, dtype=F32):
    return jax.ShapeDtypeStruct(shape, dtype)


def shifted(block, axis, distance):
    devices = range(lax.axis_size(axis))
    route = [(i - distance, i) for i in devices if i - distance in devices]
    return lax.ppermute(block, axis, route)


def splat_kernel(devices, cap, vel, wgt, off, owner, brick, send, send_brick, slot, cnt, stage):
    @pl.loop(0, devices)
    def _(d):
        cnt[d] = 0

    @pl.loop(0, devices * cap)
    def _(s):
        send_brick[s] = -1

    cell = lax.broadcasted_iota(I32, (LANES, LANES), 0)

    @pl.loop(0, wgt.shape[0] // SUB)
    def _(group):
        base = pl.multiple_of(group * SUB, SUB)
        rows = pl.ds(base, SUB)
        w = wgt[rows, :]
        for c in range(4):
            value = w if c == 3 else vel[c, rows, :] * w
            high = value.astype(jnp.bfloat16).astype(F32)
            stage[c * SUB : (c + 1) * SUB, :] = high
            stage[(c + 4) * SUB : (c + 5) * SUB, :] = value - high
        for j in range(SUB):
            lhs = stage[pl.ds(j, SUB, stride=SUB), :].astype(jnp.bfloat16)
            where = off[pl.ds(base + j, 1), :]
            hit = (cell == where).astype(F32).astype(jnp.bfloat16)
            sums = lax.dot_general(
                lhs, hit, (((1,), (1,)), ((), ())), preferred_element_type=F32
            )
            sums = sums[0:4] + sums[4:8]
            o = owner[base + j]
            r = cnt[o]
            cnt[o] = r + 1
            send_brick[o * cap + r] = brick[base + j]
            slot[base + j] = o * (3 * cap) + r
            for c in range(4):
                send[pl.ds(o * (4 * cap) + c * cap + r, 1), :] = sums[c : c + 1]


def grid_kernel(devices, cap, arrived, brick, count, code, g_out, r_out, d_out, ex, ey, tot, prev, uy):
    x = pl.program_id(0)
    span_y = code.shape[1]
    chunk = 4

    @pl.when(x == 0)
    def _():
        piece = 128

        @pl.loop(0, tot.shape[1] // piece)
        def _(i):
            for c in range(4):
                tot[c, pl.ds(pl.multiple_of(i * piece, piece), piece), :] = jnp.zeros((piece, LANES), F32)

        prev[...] = jnp.zeros_like(prev)
        uy[0] = jnp.zeros((SUB, LANES), F32)

        @pl.loop(0, devices)
        def _(d):
            @pl.loop(0, count[d])
            def _(s):
                b = brick[d * cap + s]
                for c in range(4):
                    tot[c, pl.ds(b, 1), :] += arrived[pl.ds(d * (4 * cap) + c * cap + s, 1), :]

    lane = lax.broadcasted_iota(I32, (chunk, SUB, LANES), 2)

    @pl.loop(0, span_y // chunk)
    def _(k):
        y = k * chunk
        rows = pl.ds(pl.multiple_of((x * span_y + y) * SUB, SUB), chunk * SUB)
        strips = pl.ds(y, chunk)
        kind = code[0, strips]
        inverse = 1.0 / (tot[3, rows, :].reshape(chunk, SUB, LANES) + 1.0)
        moved = []
        for a in range(3):
            face = ((kind >> a) & 1).astype(F32)
            guess = tot[a, rows, :].reshape(chunk, SUB, LANES) * inverse
            g_out[a, 0, strips] = guess
            r_out[a, 0, strips] = face * inverse
            moved.append(face * guess)
        ux, v, uz = moved
        uy[pl.ds(y + 1, chunk)] = v
        turned = pltpu.roll(uz, 1, 2)
        before = jnp.where(lane == 0, pltpu.roll(turned, 1, 1), turned)
        spread = ux - prev[strips]
        spread = spread + (v - uy[strips])
        spread = spread + (uz - before)
        d_out[0, strips] = spread
        prev[strips] = ux

    ey[0, 0] = uy[span_y]
    ex[...] = prev[...]


def solve_kernel(
    devices, cap, g_hbm, r_hbm, d_hbm, k_hbm, ex_hbm, ey_hbm, brick, p_out, reply,
    rx, ry, rz, div, kind, g, hx, hy, p1, p2, p3, here, out_sem, send_sem, recv_sem,
):
    span_x, span_y = div.shape[0], div.shape[1]
    chunk = 4
    n_slab, n_sub = lax.axis_size("slab"), lax.axis_size("sub")
    slab, sub = lax.axis_index("slab"), lax.axis_index("sub")
    east, west = lax.rem(slab + 1, n_slab), lax.rem(slab + n_slab - 1, n_slab)
    north, south = lax.rem(sub + 1, n_sub), lax.rem(sub + n_sub - 1, n_sub)
    locals_ = [
        pltpu.make_async_copy(src, dst, here.at[i])
        for i, (src, dst) in enumerate(
            [
                (d_hbm, div),
                (k_hbm, kind),
                (r_hbm.at[0], rx.at[pl.ds(1, span_x)]),
                (r_hbm.at[1], ry.at[:, pl.ds(1, span_y)]),
                (r_hbm.at[2], rz),
                (g_hbm, g),
            ]
        )
    ]
    for copy in locals_:
        copy.start()
    barrier = pltpu.get_barrier_semaphore()
    for axis, peer in (("slab", east), ("slab", west), ("sub", north), ("sub", south)):
        pl.semaphore_signal(barrier, inc=1, device_id={axis: peer}, device_id_type=MESH)
    pl.semaphore_wait(barrier, 4)

    def remote(index, src, dst, axis, peer):
        return pltpu.make_async_remote_copy(
            src_ref=src, dst_ref=dst, send_sem=send_sem.at[index], recv_sem=recv_sem.at[index],
            device_id={axis: peer}, device_id_type=MESH,
        )

    edges = [
        remote(0, ex_hbm, hx, "slab", east),
        remote(1, ey_hbm.at[:, 0], hy, "sub", north),
        remote(2, r_hbm.at[0, span_x - 1], rx.at[0], "slab", east),
        remote(3, r_hbm.at[1, :, span_y - 1], ry.at[:, 0], "sub", north),
    ]
    for copy in edges:
        copy.start()

    xs, ys = pl.ds(1, span_x), pl.ds(1, span_y)

    def x_halo(field, first, both):
        copies = [remote(first, field.at[1, ys], field.at[span_x + 1, ys], "slab", west)]
        if both:
            copies.append(remote(first + 1, field.at[span_x, ys], field.at[0, ys], "slab", east))
        return copies

    def y_halo(field, first, both):
        copies = [remote(first, field.at[xs, 1], field.at[xs, span_y + 1], "sub", south)]
        if both:
            copies.append(remote(first + 1, field.at[xs, span_y], field.at[xs, 0], "sub", north))
        return copies

    lane = lax.broadcasted_iota(I32, (chunk, SUB, LANES), 2)

    def onward(value):
        turned = pltpu.roll(value, LANES - 1, 2)
        return jnp.where(lane == LANES - 1, pltpu.roll(turned, SUB - 1, 1), turned)

    def back(value):
        turned = pltpu.roll(value, 1, 2)
        return jnp.where(lane == 0, pltpu.roll(turned, 1, 1), turned)

    def layer(x, body):
        @pl.loop(0, span_y // chunk)
        def _(k):
            body(x, k * chunk)

    def sweep(field, body, first, both):
        layer(0, body)
        layer(span_x - 1, body)
        copies = x_halo(field, first, both)
        for copy in copies:
            copy.start()

        @pl.loop(1, span_x - 1)
        def _(x):
            layer(x, body)

        later = y_halo(field, first + 2, both)
        for copy in later:
            copy.start()
        for copy in copies + later:
            copy.wait()

    def lifted(x, y, raised):
        wet = kind[x, pl.ds(y, chunk)] >= 8
        return jnp.where(wet, jnp.maximum(raised, 0.0), 0.0)

    for i in (0, 1):
        locals_[i].wait()
    for copy in edges:
        copy.wait()
    first_x = (slab > 0).astype(F32)
    first_y = (sub > 0).astype(F32)

    @pl.loop(0, span_y)
    def _(y):
        div[0, y] = div[0, y] - first_x * hx[y]
        rx[0, y] = first_x * rx[0, y]

    @pl.loop(0, span_x)
    def _(x):
        div[x, 0] = div[x, 0] - first_y * hy[x]
        ry[x, 0] = first_y * ry[x, 0]

    def start(x, y):
        p1[x + 1, pl.ds(y + 1, chunk)] = lifted(x, y, -step_size * div[x, pl.ds(y, chunk)])

    sweep(p1, start, 4, True)
    for i in (2, 3, 4):
        locals_[i].wait()

    def ascend(old, new):
        def body(x, y):
            strips, inner = pl.ds(y, chunk), pl.ds(y + 1, chunk)
            p = old[x + 1, inner]
            flow = rz[x, strips] * (p - onward(p))
            spread = div[x, strips] + (flow - back(flow))
            spread = spread + rx[x + 1, strips] * (p - old[x + 2, inner])
            spread = spread - rx[x, strips] * (old[x, inner] - p)
            spread = spread + ry[x, inner] * (p - old[x + 1, pl.ds(y + 2, chunk)])
            spread = spread - ry[x, strips] * (old[x + 1, strips] - p)
            new[x + 1, inner] = lifted(x, y, p - step_size * spread)

        return body

    sweep(p2, ascend(p1, p2), 8, True)
    sweep(p3, ascend(p2, p3), 12, False)
    locals_[5].wait()
    leave = pltpu.make_async_copy(p3, p_out, out_sem)
    leave.start()

    @pl.loop(0, span_x)
    def _(x):
        def body(x, y):
            strips, inner = pl.ds(y, chunk), pl.ds(y + 1, chunk)
            p = p3[x + 1, inner]
            after = (p3[x + 2, inner], p3[x + 1, pl.ds(y + 2, chunk)], onward(p))
            link = (rx[x + 1, strips], ry[x, inner], rz[x, strips])
            for a in range(3):
                shut = jnp.where(link[a] > 0.0, 0.0, -g[a, x, strips])
                g[a, x, strips] = shut + link[a] * (p - after[a])

        layer(x, body)

    per_layer = span_y * SUB

    @pl.loop(0, devices)
    def _(d):
        @pl.loop(0, cap)
        def _(s):
            b = jnp.maximum(brick[d * cap + s], 0)
            for a in range(3):
                row = g[a, b // per_layer, (b // SUB) % span_y, pl.ds(b % SUB, 1), :]
                reply[d * 3 + a, pl.ds(s, 1), :] = row

    leave.wait()


def face_kernel(g, r, p_here, p_next, u_out, p_out, stage):
    span_y = g.shape[2]
    lane = lax.broadcasted_iota(I32, (SUB, SUB, LANES), 2)

    @pl.loop(0, span_y // SUB)
    def _(k):
        y = pl.multiple_of(k * SUB, SUB)
        strips, inner = pl.ds(y, SUB), pl.ds(y + 1, SUB)
        p = p_here[0, inner]
        turned = pltpu.roll(p, LANES - 1, 2)
        up = jnp.where(lane == LANES - 1, pltpu.roll(turned, SUB - 1, 1), turned)
        after = (p_next[0, inner], p_here[0, pl.ds(y + 2, SUB)], up)
        stage[3] = p.reshape(SUB * SUB, LANES)
        for a in range(3):
            link = r[a, 0, strips]
            face = jnp.where(link > 0.0, g[a, 0, strips] + link * (p - after[a]), 0.0)
            stage[a] = face.reshape(SUB * SUB, LANES)
        for z in range(SUB):
            cols = slice(z * LANES, (z + 1) * LANES)
            pick = pl.ds(z, SUB, stride=SUB)
            p_out[0, strips, cols] = stage[3, pick, :]
            for a in range(3):
                u_out[a, 0, strips, cols] = stage[a, pick, :]


def gather_kernel(cap, vel, off, slot, back, out, stage):
    @pl.loop(0, off.shape[0] // SUB)
    def _(group):
        base = pl.multiple_of(group * SUB, SUB)
        rows = pl.ds(base, SUB)
        for j in range(SUB):
            s = slot[base + j]
            for c in range(3):
                stage[pl.ds(c * SUB + j, 1), :] = back[pl.ds(s + c * cap, 1), :]
        where = off[rows, :]
        for c in range(3):
            picked = jnp.take_along_axis(
                stage[c * SUB : (c + 1) * SUB, :], where, axis=1, mode="promise_in_bounds"
            )
            out[c, rows, :] = vel[c, rows, :] + picked


def on_device(velocity, weight, offset, owner, brick, flags):
    devices = lax.axis_size("slab") * lax.axis_size("sub")
    blocks = velocity.shape[0]
    cap = 2 * blocks // devices
    span_x, span_y, span_z = flags.shape
    bricks = span_x * span_y * span_z // LANES
    params = functools.partial(pltpu.CompilerParams, vmem_limit_bytes=VMEM_LIMIT)
    vel = velocity.transpose(1, 0, 2)
    grid4 = (span_x, span_y, SUB, LANES)

    open_cell = (flags != 2).astype(F32)
    wall_x = shifted(open_cell[:1], "slab", -1)
    wall_y = shifted(open_cell[:, :1], "sub", -1)

    send, send_brick, slot = pl.pallas_call(
        functools.partial(splat_kernel, devices, cap),
        out_shape=(
            struct((devices * 4 * cap, LANES)),
            struct((devices * cap,), I32),
            struct((blocks,), I32),
        ),
        in_specs=[vmem(), vmem(), vmem(), smem(), smem()],
        out_specs=(vmem(), smem(), smem()),
        scratch_shapes=[pltpu.SMEM((devices,), I32), pltpu.VMEM((8 * SUB, LANES), F32)],
        compiler_params=params(),
        name="splat",
    )(vel, weight, offset, owner[:, 0], brick[:, 0])

    exchange = functools.partial(
        lax.all_to_all, axis_name=("slab", "sub"), split_axis=0, concat_axis=0, tiled=True
    )
    arrived_brick = exchange(send_brick.reshape(devices, cap))
    arrived = exchange(send.reshape(devices, 4 * cap, LANES))
    count = jnp.sum((arrived_brick >= 0).astype(I32), axis=1)
    arrived_brick = arrived_brick.reshape(devices * cap)

    is_open = flags != 2
    next_x = jnp.concatenate([is_open[1:], wall_x > 0.0], 0)
    next_y = jnp.concatenate([is_open[:, 1:], wall_y > 0.0], 1)
    next_z = jnp.concatenate([is_open[:, :, 1:], jnp.zeros((span_x, span_y, 1), bool)], 2)
    code = (
        (is_open & next_x).astype(I32)
        + 2 * (is_open & next_y).astype(I32)
        + 4 * (is_open & next_z).astype(I32)
        + 8 * (flags == 1).astype(I32)
    ).reshape(grid4)

    whole = lambda *shape: pl.BlockSpec(shape, lambda x: (0,) * len(shape))
    one_layer = pl.BlockSpec((1, span_y, SUB, LANES), lambda x: (x, 0, 0, 0))
    three = pl.BlockSpec((3, 1, span_y, SUB, LANES), lambda x: (0, x, 0, 0, 0))
    g, r, div, edge_x, edge_y = pl.pallas_call(
        functools.partial(grid_kernel, devices, cap),
        grid=(span_x,),
        out_shape=(
            struct((3,) + grid4),
            struct((3,) + grid4),
            struct(grid4),
            struct((span_y, SUB, LANES)),
            struct((span_x, 1, SUB, LANES)),
        ),
        in_specs=[whole(devices * 4 * cap, LANES), smem(), smem(), one_layer],
        out_specs=(
            three,
            three,
            one_layer,
            whole(span_y, SUB, LANES),
            pl.BlockSpec((1, 1, SUB, LANES), lambda x: (x, 0, 0, 0)),
        ),
        scratch_shapes=[
            pltpu.VMEM((4, bricks, LANES), F32),
            pltpu.VMEM((span_y, SUB, LANES), F32),
            pltpu.VMEM((span_y + 1, SUB, LANES), F32),
        ],
        compiler_params=params(dimension_semantics=("arbitrary",)),
        name="grid",
    )(arrived.reshape(devices * 4 * cap, LANES), arrived_brick, count, code)

    padded = (span_x + 2, span_y + 2, SUB, LANES)
    p, reply = pl.pallas_call(
        functools.partial(solve_kernel, devices, cap),
        out_shape=(struct(padded), struct((devices * 3, cap, LANES))),
        in_specs=[anywhere()] * 6 + [smem()],
        out_specs=(anywhere(), vmem()),
        scratch_shapes=[
            pltpu.VMEM((span_x + 1, span_y, SUB, LANES), F32),
            pltpu.VMEM((span_x, span_y + 1, SUB, LANES), F32),
            pltpu.VMEM(grid4, F32),
            pltpu.VMEM(grid4, F32),
            pltpu.VMEM(grid4, I32),
            pltpu.VMEM((3,) + grid4, F32),
            pltpu.VMEM((span_y, SUB, LANES), F32),
            pltpu.VMEM((span_x, SUB, LANES), F32),
            pltpu.VMEM(padded, F32),
            pltpu.VMEM(padded, F32),
            pltpu.VMEM(padded, F32),
            pltpu.SemaphoreType.DMA((6,)),
            pltpu.SemaphoreType.DMA,
            pltpu.SemaphoreType.DMA((16,)),
            pltpu.SemaphoreType.DMA((16,)),
        ],
        compiler_params=params(collective_id=0, has_side_effects=True),
        name="solve",
    )(g, r, div, code, edge_x, edge_y, arrived_brick)

    returned = exchange(reply.reshape(devices, 3 * cap, LANES))

    solved, pressure = pl.pallas_call(
        face_kernel,
        grid=(span_x,),
        out_shape=(struct((3,) + flags.shape), struct(flags.shape)),
        in_specs=[
            three,
            three,
            pl.BlockSpec((1, span_y + 2, SUB, LANES), lambda x: (x + 1, 0, 0, 0)),
            pl.BlockSpec((1, span_y + 2, SUB, LANES), lambda x: (x + 2, 0, 0, 0)),
        ],
        out_specs=(
            pl.BlockSpec((3, 1, span_y, span_z), lambda x: (0, x, 0, 0)),
            pl.BlockSpec((1, span_y, span_z), lambda x: (x, 0, 0)),
        ),
        scratch_shapes=[pltpu.VMEM((4, SUB * SUB, LANES), F32)],
        compiler_params=params(dimension_semantics=("arbitrary",)),
        cost_estimate=pl.CostEstimate(flops=10**7, bytes_accessed=24 * 10**6, transcendentals=0),
        name="faces",
    )(g, r, p, p)

    updated = pl.pallas_call(
        functools.partial(gather_kernel, cap),
        out_shape=struct((3, blocks, LANES)),
        in_specs=[vmem(), vmem(), smem(), vmem()],
        out_specs=vmem(),
        scratch_shapes=[pltpu.VMEM((3 * SUB, LANES), F32)],
        compiler_params=params(),
        name="gather",
    )(vel, offset, slot, returned.reshape(devices * 3 * cap, LANES))
    return updated.transpose(1, 0, 2), pressure, solved


def solution(mesh):
    in_specs = (
        P(("slab", "sub"), None, None),
        P(("slab", "sub"), None),
        P(("slab", "sub"), None),
        P(("slab", "sub"), None),
        P(("slab", "sub"), None),
        P("slab", "sub", None),
    )
    out_specs = (
        P(("slab", "sub"), None, None),
        P("slab", "sub", None),
        P(None, "slab", "sub", None),
    )
    return jax.shard_map(
        on_device, mesh=mesh, in_specs=in_specs, out_specs=out_specs, check_vma=False
    )
```

```python
import functools

import jax
import jax.numpy as jnp
from jax import lax
from jax.experimental import pallas as pl
from jax.experimental.pallas import tpu as pltpu
from jax.sharding import PartitionSpec as P

LANES = 128
SUB = 8
ITERS = 3

step_size = 0.15
MESH = pl.DeviceIdType.MESH
F32 = jnp.float32
I32 = jnp.int32
VMEM_LIMIT = 60 * 1024 * 1024


def vmem():
    return pl.BlockSpec(memory_space=pltpu.VMEM)


def smem():
    return pl.BlockSpec(memory_space=pltpu.SMEM)


def anywhere():
    return pl.BlockSpec(memory_space=pl.ANY)


def struct(shape, dtype=F32):
    return jax.ShapeDtypeStruct(shape, dtype)


def shifted(block, axis, distance):
    devices = range(lax.axis_size(axis))
    route = [(i - distance, i) for i in devices if i - distance in devices]
    return lax.ppermute(block, axis, route)


def splat_kernel(devices, cap, vel, wgt, off, owner, brick, send, slot, cnt, stage):
    @pl.loop(0, devices)
    def _(d):
        cnt[d] = 0

    stride = 4 * cap + SUB

    @pl.loop(0, devices)
    def _(d):
        tags = pl.multiple_of(d * stride + 4 * cap, SUB)
        send[pl.ds(tags, SUB), :] = jnp.full((SUB, LANES), -1.0, F32)

    lane = lax.broadcasted_iota(I32, (1, LANES), 1)
    cell = lax.broadcasted_iota(I32, (LANES, LANES), 0)

    @pl.loop(0, wgt.shape[0] // SUB)
    def _(group):
        base = pl.multiple_of(group * SUB, SUB)
        rows = pl.ds(base, SUB)
        w = wgt[rows, :]
        for c in range(4):
            value = w if c == 3 else vel[c, rows, :] * w
            high = value.astype(jnp.bfloat16).astype(F32)
            stage[c * SUB : (c + 1) * SUB, :] = high
            stage[(c + 4) * SUB : (c + 5) * SUB, :] = value - high
        for j in range(SUB):
            lhs = stage[pl.ds(j, SUB, stride=SUB), :].astype(jnp.bfloat16)
            where = off[pl.ds(base + j, 1), :]
            hit = (cell == where).astype(F32).astype(jnp.bfloat16)
            sums = lax.dot_general(
                lhs, hit, (((1,), (1,)), ((), ())), preferred_element_type=F32
            )
            sums = sums[0:4] + sums[4:8]
            o = owner[base + j]
            r = cnt[o]
            cnt[o] = r + 1
            tags = pl.ds(o * stride + 4 * cap, 1)
            send[tags, :] = jnp.where(lane == r, brick[base + j].astype(F32), send[tags, :])
            slot[base + j] = o * (3 * cap) + r
            for c in range(4):
                send[pl.ds(o * stride + c * cap + r, 1), :] = sums[c : c + 1]


def grid_kernel(devices, cap, arrived, brick, count, code, g_out, r_out, d_out, ex, ey, tot, prev, uy):
    x = pl.program_id(0)
    span_y = code.shape[1]
    chunk = 4

    @pl.when(x == 0)
    def _():
        piece = 128

        @pl.loop(0, tot.shape[1] // piece)
        def _(i):
            for c in range(4):
                tot[c, pl.ds(pl.multiple_of(i * piece, piece), piece), :] = jnp.zeros((piece, LANES), F32)

        prev[...] = jnp.zeros_like(prev)
        uy[0] = jnp.zeros((SUB, LANES), F32)

        @pl.loop(0, devices)
        def _(d):
            @pl.loop(0, count[d])
            def _(s):
                b = brick[d * cap + s]
                for c in range(4):
                    tot[c, pl.ds(b, 1), :] += arrived[pl.ds(d * (4 * cap + SUB) + c * cap + s, 1), :]

    lane = lax.broadcasted_iota(I32, (chunk, SUB, LANES), 2)

    @pl.loop(0, span_y // chunk)
    def _(k):
        y = k * chunk
        rows = pl.ds(pl.multiple_of((x * span_y + y) * SUB, SUB), chunk * SUB)
        strips = pl.ds(y, chunk)
        kind = code[0, strips]
        inverse = 1.0 / (tot[3, rows, :].reshape(chunk, SUB, LANES) + 1.0)
        moved = []
        for a in range(3):
            face = ((kind >> a) & 1).astype(F32)
            guess = tot[a, rows, :].reshape(chunk, SUB, LANES) * inverse
            g_out[a, 0, strips] = guess
            r_out[a, 0, strips] = face * inverse
            moved.append(face * guess)
        ux, v, uz = moved
        uy[pl.ds(y + 1, chunk)] = v
        turned = pltpu.roll(uz, 1, 2)
        before = jnp.where(lane == 0, pltpu.roll(turned, 1, 1), turned)
        spread = ux - prev[strips]
        spread = spread + (v - uy[strips])
        spread = spread + (uz - before)
        d_out[0, strips] = spread
        prev[strips] = ux

    ey[0, 0] = uy[span_y]
    ex[...] = prev[...]


def solve_kernel(
    devices, cap, g_hbm, r_hbm, d_hbm, k_hbm, ex_hbm, ey_hbm, brick, p_out, reply,
    rx, ry, rz, div, kind, g, hx, hy, p1, p2, p3, here, out_sem, send_sem, recv_sem,
):
    span_x, span_y = div.shape[0], div.shape[1]
    chunk = 4
    n_slab, n_sub = lax.axis_size("slab"), lax.axis_size("sub")
    slab, sub = lax.axis_index("slab"), lax.axis_index("sub")
    east, west = lax.rem(slab + 1, n_slab), lax.rem(slab + n_slab - 1, n_slab)
    north, south = lax.rem(sub + 1, n_sub), lax.rem(sub + n_sub - 1, n_sub)
    locals_ = [
        pltpu.make_async_copy(src, dst, here.at[i])
        for i, (src, dst) in enumerate(
            [
                (d_hbm, div),
                (k_hbm, kind),
                (r_hbm.at[0], rx.at[pl.ds(1, span_x)]),
                (r_hbm.at[1], ry.at[:, pl.ds(1, span_y)]),
                (r_hbm.at[2], rz),
                (g_hbm, g),
            ]
        )
    ]
    for copy in locals_:
        copy.start()
    barrier = pltpu.get_barrier_semaphore()
    for axis, peer in (("slab", east), ("slab", west), ("sub", north), ("sub", south)):
        pl.semaphore_signal(barrier, inc=1, device_id={axis: peer}, device_id_type=MESH)
    pl.semaphore_wait(barrier, 4)

    def remote(index, src, dst, axis, peer):
        return pltpu.make_async_remote_copy(
            src_ref=src, dst_ref=dst, send_sem=send_sem.at[index], recv_sem=recv_sem.at[index],
            device_id={axis: peer}, device_id_type=MESH,
        )

    edges = [
        remote(0, ex_hbm, hx, "slab", east),
        remote(1, ey_hbm.at[:, 0], hy, "sub", north),
        remote(2, r_hbm.at[0, span_x - 1], rx.at[0], "slab", east),
        remote(3, r_hbm.at[1, :, span_y - 1], ry.at[:, 0], "sub", north),
    ]
    for copy in edges:
        copy.start()

    xs, ys = pl.ds(1, span_x), pl.ds(1, span_y)

    def x_halo(field, first, both):
        copies = [remote(first, field.at[1, ys], field.at[span_x + 1, ys], "slab", west)]
        if both:
            copies.append(remote(first + 1, field.at[span_x, ys], field.at[0, ys], "slab", east))
        return copies

    def y_halo(field, first, both):
        copies = [remote(first, field.at[xs, 1], field.at[xs, span_y + 1], "sub", south)]
        if both:
            copies.append(remote(first + 1, field.at[xs, span_y], field.at[xs, 0], "sub", north))
        return copies

    lane = lax.broadcasted_iota(I32, (chunk, SUB, LANES), 2)

    def onward(value):
        turned = pltpu.roll(value, LANES - 1, 2)
        return jnp.where(lane == LANES - 1, pltpu.roll(turned, SUB - 1, 1), turned)

    def back(value):
        turned = pltpu.roll(value, 1, 2)
        return jnp.where(lane == 0, pltpu.roll(turned, 1, 1), turned)

    def layer(x, body):
        @pl.loop(0, span_y // chunk)
        def _(k):
            body(x, k * chunk)

    def sweep(field, body, first, both):
        layer(0, body)
        layer(span_x - 1, body)
        copies = x_halo(field, first, both)
        for copy in copies:
            copy.start()

        @pl.loop(1, span_x - 1)
        def _(x):
            layer(x, body)

        later = y_halo(field, first + 2, both)
        for copy in later:
            copy.start()
        for copy in copies + later:
            copy.wait()

    def lifted(x, y, raised):
        wet = kind[x, pl.ds(y, chunk)] >= 8
        return jnp.where(wet, jnp.maximum(raised, 0.0), 0.0)

    for i in (0, 1):
        locals_[i].wait()
    for copy in edges:
        copy.wait()
    first_x = (slab > 0).astype(F32)
    first_y = (sub > 0).astype(F32)

    @pl.loop(0, span_y)
    def _(y):
        div[0, y] = div[0, y] - first_x * hx[y]
        rx[0, y] = first_x * rx[0, y]

    @pl.loop(0, span_x)
    def _(x):
        div[x, 0] = div[x, 0] - first_y * hy[x]
        ry[x, 0] = first_y * ry[x, 0]

    def start(x, y):
        p1[x + 1, pl.ds(y + 1, chunk)] = lifted(x, y, -step_size * div[x, pl.ds(y, chunk)])

    sweep(p1, start, 4, True)
    for i in (2, 3, 4):
        locals_[i].wait()

    def ascend(old, new):
        def body(x, y):
            strips, inner = pl.ds(y, chunk), pl.ds(y + 1, chunk)
            p = old[x + 1, inner]
            flow = rz[x, strips] * (p - onward(p))
            spread = div[x, strips] + (flow - back(flow))
            spread = spread + rx[x + 1, strips] * (p - old[x + 2, inner])
            spread = spread - rx[x, strips] * (old[x, inner] - p)
            spread = spread + ry[x, inner] * (p - old[x + 1, pl.ds(y + 2, chunk)])
            spread = spread - ry[x, strips] * (old[x + 1, strips] - p)
            new[x + 1, inner] = lifted(x, y, p - step_size * spread)

        return body

    sweep(p2, ascend(p1, p2), 8, True)
    sweep(p3, ascend(p2, p3), 12, False)
    locals_[5].wait()
    leave = pltpu.make_async_copy(p3, p_out, out_sem)
    leave.start()

    @pl.loop(0, span_x)
    def _(x):
        def body(x, y):
            strips, inner = pl.ds(y, chunk), pl.ds(y + 1, chunk)
            rows = pl.ds(pl.multiple_of((x * span_y + y) * SUB, SUB), chunk * SUB)
            p = p3[x + 1, inner]
            after = (p3[x + 2, inner], p3[x + 1, pl.ds(y + 2, chunk)], onward(p))
            link = (rx[x + 1, strips], ry[x, inner], rz[x, strips])
            for a in range(3):
                shut = jnp.where(link[a] > 0.0, 0.0, -g[a, rows, :].reshape(chunk, SUB, LANES))
                change = shut + link[a] * (p - after[a])
                g[a, rows, :] = change.reshape(chunk * SUB, LANES)

        layer(x, body)

    @pl.loop(0, devices)
    def _(d):
        @pl.loop(0, cap, unroll=8)
        def _(s):
            b = jnp.maximum(brick[d * cap + s], 0)
            for a in range(3):
                reply[pl.ds(d * (3 * cap) + a * cap + s, 1), :] = g[a, pl.ds(b, 1), :]

    leave.wait()


def face_kernel(g, r, p_here, p_next, u_out, p_out, stage):
    span_y = g.shape[2]
    lane = lax.broadcasted_iota(I32, (SUB, SUB, LANES), 2)

    @pl.loop(0, span_y // SUB)
    def _(k):
        y = pl.multiple_of(k * SUB, SUB)
        strips, inner = pl.ds(y, SUB), pl.ds(y + 1, SUB)
        p = p_here[0, inner]
        turned = pltpu.roll(p, LANES - 1, 2)
        up = jnp.where(lane == LANES - 1, pltpu.roll(turned, SUB - 1, 1), turned)
        after = (p_next[0, inner], p_here[0, pl.ds(y + 2, SUB)], up)
        stage[3] = p.reshape(SUB * SUB, LANES)
        for a in range(3):
            link = r[a, 0, strips]
            face = jnp.where(link > 0.0, g[a, 0, strips] + link * (p - after[a]), 0.0)
            stage[a] = face.reshape(SUB * SUB, LANES)
        for z in range(SUB):
            cols = slice(z * LANES, (z + 1) * LANES)
            pick = pl.ds(z, SUB, stride=SUB)
            p_out[0, strips, cols] = stage[3, pick, :]
            for a in range(3):
                u_out[a, 0, strips, cols] = stage[a, pick, :]


def gather_kernel(cap, vel, off, slot, back, out, stage):
    @pl.loop(0, off.shape[0] // SUB)
    def _(group):
        base = pl.multiple_of(group * SUB, SUB)
        rows = pl.ds(base, SUB)
        for j in range(SUB):
            s = slot[base + j]
            for c in range(3):
                stage[pl.ds(c * SUB + j, 1), :] = back[pl.ds(s + c * cap, 1), :]
        where = off[rows, :]
        for c in range(3):
            picked = jnp.take_along_axis(
                stage[c * SUB : (c + 1) * SUB, :], where, axis=1, mode="promise_in_bounds"
            )
            out[c, rows, :] = vel[c, rows, :] + picked


def on_device(velocity, weight, offset, owner, brick, flags):
    devices = lax.axis_size("slab") * lax.axis_size("sub")
    blocks = velocity.shape[0]
    cap = 2 * blocks // devices
    span_x, span_y, span_z = flags.shape
    bricks = span_x * span_y * span_z // LANES
    params = functools.partial(pltpu.CompilerParams, vmem_limit_bytes=VMEM_LIMIT)
    vel = velocity.transpose(1, 0, 2)
    grid4 = (span_x, span_y, SUB, LANES)

    open_cell = (flags != 2).astype(F32)
    wall_x = shifted(open_cell[:1], "slab", -1)
    wall_y = shifted(open_cell[:, :1], "sub", -1)

    stride = 4 * cap + SUB
    send, slot = pl.pallas_call(
        functools.partial(splat_kernel, devices, cap),
        out_shape=(
            struct((devices * stride, LANES)),
            struct((blocks,), I32),
        ),
        in_specs=[vmem(), vmem(), vmem(), smem(), smem()],
        out_specs=(vmem(), smem()),
        scratch_shapes=[pltpu.SMEM((devices,), I32), pltpu.VMEM((8 * SUB, LANES), F32)],
        compiler_params=params(),
        name="splat",
    )(vel, weight, offset, owner[:, 0], brick[:, 0])

    exchange = functools.partial(
        lax.all_to_all, axis_name=("slab", "sub"), split_axis=0, concat_axis=0, tiled=True
    )
    arrived = exchange(send.reshape(devices, stride, LANES))
    arrived_brick = arrived[:, 4 * cap, :cap].astype(I32)
    count = jnp.sum((arrived_brick >= 0).astype(I32), axis=1)
    arrived_brick = arrived_brick.reshape(devices * cap)

    is_open = flags != 2
    next_x = jnp.concatenate([is_open[1:], wall_x > 0.0], 0)
    next_y = jnp.concatenate([is_open[:, 1:], wall_y > 0.0], 1)
    next_z = jnp.concatenate([is_open[:, :, 1:], jnp.zeros((span_x, span_y, 1), bool)], 2)
    code = (
        (is_open & next_x).astype(I32)
        + 2 * (is_open & next_y).astype(I32)
        + 4 * (is_open & next_z).astype(I32)
        + 8 * (flags == 1).astype(I32)
    ).reshape(grid4)

    whole = lambda *shape: pl.BlockSpec(shape, lambda x: (0,) * len(shape))
    one_layer = pl.BlockSpec((1, span_y, SUB, LANES), lambda x: (x, 0, 0, 0))
    three = pl.BlockSpec((3, 1, span_y, SUB, LANES), lambda x: (0, x, 0, 0, 0))
    g, r, div, edge_x, edge_y = pl.pallas_call(
        functools.partial(grid_kernel, devices, cap),
        grid=(span_x,),
        out_shape=(
            struct((3,) + grid4),
            struct((3,) + grid4),
            struct(grid4),
            struct((span_y, SUB, LANES)),
            struct((span_x, 1, SUB, LANES)),
        ),
        in_specs=[whole(devices * stride, LANES), smem(), smem(), one_layer],
        out_specs=(
            three,
            three,
            one_layer,
            whole(span_y, SUB, LANES),
            pl.BlockSpec((1, 1, SUB, LANES), lambda x: (x, 0, 0, 0)),
        ),
        scratch_shapes=[
            pltpu.VMEM((4, bricks, LANES), F32),
            pltpu.VMEM((span_y, SUB, LANES), F32),
            pltpu.VMEM((span_y + 1, SUB, LANES), F32),
        ],
        compiler_params=params(dimension_semantics=("arbitrary",)),
        name="grid",
    )(arrived.reshape(devices * stride, LANES), arrived_brick, count, code)

    padded = (span_x + 2, span_y + 2, SUB, LANES)
    p, reply = pl.pallas_call(
        functools.partial(solve_kernel, devices, cap),
        out_shape=(struct(padded), struct((devices * 3 * cap, LANES))),
        in_specs=[anywhere()] * 6 + [smem()],
        out_specs=(anywhere(), vmem()),
        scratch_shapes=[
            pltpu.VMEM((span_x + 1, span_y, SUB, LANES), F32),
            pltpu.VMEM((span_x, span_y + 1, SUB, LANES), F32),
            pltpu.VMEM(grid4, F32),
            pltpu.VMEM(grid4, F32),
            pltpu.VMEM(grid4, I32),
            pltpu.VMEM((3, bricks, LANES), F32),
            pltpu.VMEM((span_y, SUB, LANES), F32),
            pltpu.VMEM((span_x, SUB, LANES), F32),
            pltpu.VMEM(padded, F32),
            pltpu.VMEM(padded, F32),
            pltpu.VMEM(padded, F32),
            pltpu.SemaphoreType.DMA((6,)),
            pltpu.SemaphoreType.DMA,
            pltpu.SemaphoreType.DMA((16,)),
            pltpu.SemaphoreType.DMA((16,)),
        ],
        compiler_params=params(collective_id=0, has_side_effects=True),
        name="solve",
    )(g.reshape(3, bricks, LANES), r, div, code, edge_x, edge_y, arrived_brick)

    returned = exchange(reply.reshape(devices, 3 * cap, LANES))

    solved, pressure = pl.pallas_call(
        face_kernel,
        grid=(span_x,),
        out_shape=(struct((3,) + flags.shape), struct(flags.shape)),
        in_specs=[
            three,
            three,
            pl.BlockSpec((1, span_y + 2, SUB, LANES), lambda x: (x + 1, 0, 0, 0)),
            pl.BlockSpec((1, span_y + 2, SUB, LANES), lambda x: (x + 2, 0, 0, 0)),
        ],
        out_specs=(
            pl.BlockSpec((3, 1, span_y, span_z), lambda x: (0, x, 0, 0)),
            pl.BlockSpec((1, span_y, span_z), lambda x: (x, 0, 0)),
        ),
        scratch_shapes=[pltpu.VMEM((4, SUB * SUB, LANES), F32)],
        compiler_params=params(dimension_semantics=("arbitrary",)),
        cost_estimate=pl.CostEstimate(flops=10**7, bytes_accessed=24 * 10**6, transcendentals=0),
        name="faces",
    )(g, r, p, p)

    updated = pl.pallas_call(
        functools.partial(gather_kernel, cap),
        out_shape=struct((3, blocks, LANES)),
        in_specs=[vmem(), vmem(), smem(), vmem()],
        out_specs=vmem(),
        scratch_shapes=[pltpu.VMEM((3 * SUB, LANES), F32)],
        compiler_params=params(),
        name="gather",
    )(vel, offset, slot, returned.reshape(devices * 3 * cap, LANES))
    return updated.transpose(1, 0, 2), pressure, solved


def solution(mesh):
    in_specs = (
        P(("slab", "sub"), None, None),
        P(("slab", "sub"), None),
        P(("slab", "sub"), None),
        P(("slab", "sub"), None),
        P(("slab", "sub"), None),
        P("slab", "sub", None),
    )
    out_specs = (
        P(("slab", "sub"), None, None),
        P("slab", "sub", None),
        P(None, "slab", "sub", None),
    )
    return jax.shard_map(
        on_device, mesh=mesh, in_specs=in_specs, out_specs=out_specs, check_vma=False
    )
```

```python
import functools

import jax
import jax.numpy as jnp
from jax import lax
from jax.experimental import pallas as pl
from jax.experimental.pallas import tpu as pltpu
from jax.sharding import PartitionSpec as P

LANES = 128
SUB = 8
ITERS = 3

step_size = 0.15
MESH = pl.DeviceIdType.MESH
F32 = jnp.float32
I32 = jnp.int32
VMEM_LIMIT = 60 * 1024 * 1024


def vmem():
    return pl.BlockSpec(memory_space=pltpu.VMEM)


def smem():
    return pl.BlockSpec(memory_space=pltpu.SMEM)


def anywhere():
    return pl.BlockSpec(memory_space=pl.ANY)


def struct(shape, dtype=F32):
    return jax.ShapeDtypeStruct(shape, dtype)


def shifted(block, axis, distance):
    devices = range(lax.axis_size(axis))
    route = [(i - distance, i) for i in devices if i - distance in devices]
    return lax.ppermute(block, axis, route)


def splat_kernel(devices, cap, vel, wgt, off, owner, brick, send, slot, cnt, stage):
    @pl.loop(0, devices)
    def _(d):
        cnt[d] = 0

    stride = 4 * cap + SUB

    @pl.loop(0, devices)
    def _(d):
        tags = pl.multiple_of(d * stride + 4 * cap, SUB)
        send[pl.ds(tags, SUB), :] = jnp.full((SUB, LANES), -1.0, F32)

    lane = lax.broadcasted_iota(I32, (1, LANES), 1)
    cell = lax.broadcasted_iota(I32, (LANES, LANES), 0)

    @pl.loop(0, wgt.shape[0] // SUB)
    def _(group):
        base = pl.multiple_of(group * SUB, SUB)
        rows = pl.ds(base, SUB)
        w = wgt[rows, :]
        for c in range(4):
            value = w if c == 3 else vel[c, rows, :] * w
            high = value.astype(jnp.bfloat16).astype(F32)
            stage[c * SUB : (c + 1) * SUB, :] = high
            stage[(c + 4) * SUB : (c + 5) * SUB, :] = value - high
        for j in range(SUB):
            lhs = stage[pl.ds(j, SUB, stride=SUB), :].astype(jnp.bfloat16)
            where = off[pl.ds(base + j, 1), :]
            hit = (cell == where).astype(F32).astype(jnp.bfloat16)
            sums = lax.dot_general(
                lhs, hit, (((1,), (1,)), ((), ())), preferred_element_type=F32
            )
            sums = sums[0:4] + sums[4:8]
            o = owner[base + j]
            r = cnt[o]
            cnt[o] = r + 1
            tags = pl.ds(o * stride + 4 * cap, 1)
            send[tags, :] = jnp.where(lane == r, brick[base + j].astype(F32), send[tags, :])
            slot[base + j] = o * (3 * cap) + r
            for c in range(4):
                send[pl.ds(o * stride + c * cap + r, 1), :] = sums[c : c + 1]


def grid_kernel(devices, cap, arrived, brick, count, code, g_out, r_out, d_out, ex, ey, tot, prev, uy):
    x = pl.program_id(0)
    span_y = code.shape[1]
    chunk = 4

    @pl.when(x == 0)
    def _():
        piece = 128

        @pl.loop(0, tot.shape[1] // piece)
        def _(i):
            for c in range(4):
                tot[c, pl.ds(pl.multiple_of(i * piece, piece), piece), :] = jnp.zeros((piece, LANES), F32)

        prev[...] = jnp.zeros_like(prev)
        uy[0] = jnp.zeros((SUB, LANES), F32)

        @pl.loop(0, devices)
        def _(d):
            @pl.loop(0, count[d])
            def _(s):
                b = brick[d * cap + s]
                for c in range(4):
                    tot[c, pl.ds(b, 1), :] += arrived[pl.ds(d * (4 * cap + SUB) + c * cap + s, 1), :]

    lane = lax.broadcasted_iota(I32, (chunk, SUB, LANES), 2)

    @pl.loop(0, span_y // chunk)
    def _(k):
        y = k * chunk
        rows = pl.ds(pl.multiple_of((x * span_y + y) * SUB, SUB), chunk * SUB)
        strips = pl.ds(y, chunk)
        kind = code[0, strips]
        inverse = 1.0 / (tot[3, rows, :].reshape(chunk, SUB, LANES) + 1.0)
        moved = []
        for a in range(3):
            face = ((kind >> a) & 1).astype(F32)
            guess = tot[a, rows, :].reshape(chunk, SUB, LANES) * inverse
            g_out[a, 0, strips] = guess
            r_out[a, 0, strips] = face * inverse
            moved.append(face * guess)
        ux, v, uz = moved
        uy[pl.ds(y + 1, chunk)] = v
        turned = pltpu.roll(uz, 1, 2)
        before = jnp.where(lane == 0, pltpu.roll(turned, 1, 1), turned)
        spread = ux - prev[strips]
        spread = spread + (v - uy[strips])
        spread = spread + (uz - before)
        d_out[0, strips] = spread
        prev[strips] = ux

    ey[0, 0] = uy[span_y]
    ex[...] = prev[...]


def solve_kernel(
    devices, cap, g_hbm, r_hbm, d_hbm, k_hbm, ex_hbm, ey_hbm, brick, p_out, reply,
    rx, ry, rz, div, kind, g, hx, hy, p1, p2, p3, here, out_sem, send_sem, recv_sem,
):
    span_x, span_y = div.shape[0], div.shape[1]
    chunk = 4
    n_slab, n_sub = lax.axis_size("slab"), lax.axis_size("sub")
    slab, sub = lax.axis_index("slab"), lax.axis_index("sub")
    east, west = lax.rem(slab + 1, n_slab), lax.rem(slab + n_slab - 1, n_slab)
    north, south = lax.rem(sub + 1, n_sub), lax.rem(sub + n_sub - 1, n_sub)
    locals_ = [
        pltpu.make_async_copy(src, dst, here.at[i])
        for i, (src, dst) in enumerate(
            [
                (d_hbm, div),
                (k_hbm, kind),
                (r_hbm.at[0], rx.at[pl.ds(1, span_x)]),
                (r_hbm.at[1], ry.at[:, pl.ds(1, span_y)]),
                (r_hbm.at[2], rz),
                (g_hbm, g),
            ]
        )
    ]
    for copy in locals_:
        copy.start()
    barrier = pltpu.get_barrier_semaphore()
    for axis, peer in (("slab", east), ("slab", west), ("sub", north), ("sub", south)):
        pl.semaphore_signal(barrier, inc=1, device_id={axis: peer}, device_id_type=MESH)
    pl.semaphore_wait(barrier, 4)

    def remote(index, src, dst, axis, up):
        place, size = (slab, n_slab) if axis == "slab" else (sub, n_sub)
        after, before = place < size - 1, place > 0
        peer = {"slab": (east, west), "sub": (north, south)}[axis][0 if up else 1]
        copy = pltpu.make_async_remote_copy(
            src_ref=src, dst_ref=dst, send_sem=send_sem.at[index], recv_sem=recv_sem.at[index],
            device_id={axis: peer}, device_id_type=MESH,
        )
        return copy, (after if up else before), (before if up else after)

    def begin(*moves):
        for copy, sends, _ in moves:
            pl.when(sends)(copy.start)

    def finish(*moves):
        for copy, sends, gets in moves:
            pl.when(sends)(copy.wait_send)
            pl.when(gets)(copy.wait_recv)

    xs, ys = pl.ds(1, span_x), pl.ds(1, span_y)
    flow_x = remote(0, ex_hbm, hx, "slab", True)
    flow_y = remote(1, ey_hbm.at[:, 0], hy, "sub", True)
    link_x = remote(2, r_hbm.at[0, span_x - 1], rx.at[0], "slab", True)
    link_y = remote(3, r_hbm.at[1, :, span_y - 1], ry.at[:, 0], "sub", True)
    begin(flow_y, flow_x)

    def halos(field, first):
        return (
            remote(first, field.at[1, ys], field.at[span_x + 1, ys], "slab", False),
            remote(first + 1, field.at[span_x, ys], field.at[0, ys], "slab", True),
            remote(first + 2, field.at[xs, 1], field.at[xs, span_y + 1], "sub", False),
            remote(first + 3, field.at[xs, span_y], field.at[xs, 0], "sub", True),
        )

    nothing = jnp.zeros((SUB, LANES), F32)

    @pl.when(slab == 0)
    def _():
        @pl.loop(0, span_y)
        def _(y):
            hx[y] = nothing
            rx[0, y] = nothing
            for field in (p1, p2):
                field[0, y + 1] = nothing

    @pl.when(slab == n_slab - 1)
    def _():
        @pl.loop(0, span_y)
        def _(y):
            for field in (p1, p2, p3):
                field[span_x + 1, y + 1] = nothing

    @pl.when(sub == 0)
    def _():
        @pl.loop(0, span_x)
        def _(x):
            hy[x] = nothing
            ry[x, 0] = nothing
            for field in (p1, p2):
                field[x + 1, 0] = nothing

    @pl.when(sub == n_sub - 1)
    def _():
        @pl.loop(0, span_x)
        def _(x):
            for field in (p1, p2, p3):
                field[x + 1, span_y + 1] = nothing

    lane = lax.broadcasted_iota(I32, (chunk, SUB, LANES), 2)

    def onward(value):
        turned = pltpu.roll(value, LANES - 1, 2)
        return jnp.where(lane == LANES - 1, pltpu.roll(turned, SUB - 1, 1), turned)

    def back(value):
        turned = pltpu.roll(value, 1, 2)
        return jnp.where(lane == 0, pltpu.roll(turned, 1, 1), turned)

    def layers(low, high, body):
        @pl.loop(low, high)
        def _(x):
            @pl.loop(0, span_y // chunk)
            def _(k):
                body(x, k * chunk)

    def lifted(x, y, raised):
        wet = kind[x, pl.ds(y, chunk)] >= 8
        return jnp.where(wet, jnp.maximum(raised, 0.0), 0.0)

    def start(x, y):
        p1[x + 1, pl.ds(y + 1, chunk)] = lifted(x, y, -step_size * div[x, pl.ds(y, chunk)])

    for i in (0, 1):
        locals_[i].wait()
    finish(flow_y)

    @pl.loop(0, span_x)
    def _(x):
        div[x, 0] = div[x, 0] - hy[x]

    down, up, south_1, north_1 = halos(p1, 4)
    layers(span_x - 1, span_x, start)
    begin(up, link_x, link_y)
    layers(1, span_x - 1, start)
    finish(flow_x)

    @pl.loop(0, span_y)
    def _(y):
        div[0, y] = div[0, y] - hx[y]

    layers(0, 1, start)
    begin(down, south_1, north_1)
    for i in (2, 3, 4):
        locals_[i].wait()

    def ascend(old, new):
        def body(x, y):
            strips, inner = pl.ds(y, chunk), pl.ds(y + 1, chunk)
            p = old[x + 1, inner]
            flow = rz[x, strips] * (p - onward(p))
            spread = div[x, strips] + (flow - back(flow))
            spread = spread + rx[x + 1, strips] * (p - old[x + 2, inner])
            spread = spread - rx[x, strips] * (old[x, inner] - p)
            spread = spread + ry[x, inner] * (p - old[x + 1, pl.ds(y + 2, chunk)])
            spread = spread - ry[x, strips] * (old[x + 1, strips] - p)
            new[x + 1, inner] = lifted(x, y, p - step_size * spread)

        return body

    body = ascend(p1, p2)
    down_2, up_2, south_2, north_2 = halos(p2, 8)
    finish(link_y, south_1, north_1)
    layers(1, span_x - 1, body)
    finish(link_x, up, down)
    layers(0, 1, body)
    begin(down_2)
    layers(span_x - 1, span_x, body)
    begin(up_2, south_2, north_2)

    body = ascend(p2, p3)
    down_3, _, south_3, _ = halos(p3, 12)
    finish(south_2, north_2)
    layers(1, span_x - 1, body)
    finish(up_2, down_2)
    layers(0, 1, body)
    begin(down_3)
    layers(span_x - 1, span_x, body)
    begin(south_3)
    locals_[5].wait()

    def settle(x, y):
        strips, inner = pl.ds(y, chunk), pl.ds(y + 1, chunk)
        rows = pl.ds(pl.multiple_of((x * span_y + y) * SUB, SUB), chunk * SUB)
        p = p3[x + 1, inner]
        after = (p3[x + 2, inner], p3[x + 1, pl.ds(y + 2, chunk)], onward(p))
        link = (rx[x + 1, strips], ry[x, inner], rz[x, strips])
        for a in range(3):
            shut = jnp.where(link[a] > 0.0, 0.0, -g[a, rows, :].reshape(chunk, SUB, LANES))
            change = shut + link[a] * (p - after[a])
            g[a, rows, :] = change.reshape(chunk * SUB, LANES)

    finish(south_3)
    layers(0, span_x - 1, settle)
    finish(down_3)
    leave = pltpu.make_async_copy(p3, p_out, out_sem)
    leave.start()
    layers(span_x - 1, span_x, settle)

    @pl.loop(0, devices)
    def _(d):
        @pl.loop(0, cap, unroll=8)
        def _(s):
            b = jnp.maximum(brick[d * cap + s], 0)
            for a in range(3):
                reply[pl.ds(d * (3 * cap) + a * cap + s, 1), :] = g[a, pl.ds(b, 1), :]

    leave.wait()


def face_kernel(g, r, p_here, p_next, u_out, p_out, stage):
    span_y = g.shape[2]
    lane = lax.broadcasted_iota(I32, (SUB, SUB, LANES), 2)

    @pl.loop(0, span_y // SUB)
    def _(k):
        y = pl.multiple_of(k * SUB, SUB)
        strips, inner = pl.ds(y, SUB), pl.ds(y + 1, SUB)
        p = p_here[0, inner]
        turned = pltpu.roll(p, LANES - 1, 2)
        up = jnp.where(lane == LANES - 1, pltpu.roll(turned, SUB - 1, 1), turned)
        after = (p_next[0, inner], p_here[0, pl.ds(y + 2, SUB)], up)
        stage[3] = p.reshape(SUB * SUB, LANES)
        for a in range(3):
            link = r[a, 0, strips]
            face = jnp.where(link > 0.0, g[a, 0, strips] + link * (p - after[a]), 0.0)
            stage[a] = face.reshape(SUB * SUB, LANES)
        for z in range(SUB):
            cols = slice(z * LANES, (z + 1) * LANES)
            pick = pl.ds(z, SUB, stride=SUB)
            p_out[0, strips, cols] = stage[3, pick, :]
            for a in range(3):
                u_out[a, 0, strips, cols] = stage[a, pick, :]


def gather_kernel(cap, vel, off, slot, back, out, stage):
    @pl.loop(0, off.shape[0] // SUB)
    def _(group):
        base = pl.multiple_of(group * SUB, SUB)
        rows = pl.ds(base, SUB)
        for j in range(SUB):
            s = slot[base + j]
            for c in range(3):
                stage[pl.ds(c * SUB + j, 1), :] = back[pl.ds(s + c * cap, 1), :]
        where = off[rows, :]
        for c in range(3):
            picked = jnp.take_along_axis(
                stage[c * SUB : (c + 1) * SUB, :], where, axis=1, mode="promise_in_bounds"
            )
            out[c, rows, :] = vel[c, rows, :] + picked


def on_device(velocity, weight, offset, owner, brick, flags):
    devices = lax.axis_size("slab") * lax.axis_size("sub")
    blocks = velocity.shape[0]
    cap = 2 * blocks // devices
    span_x, span_y, span_z = flags.shape
    bricks = span_x * span_y * span_z // LANES
    params = functools.partial(pltpu.CompilerParams, vmem_limit_bytes=VMEM_LIMIT)
    vel = velocity.transpose(1, 0, 2)
    grid4 = (span_x, span_y, SUB, LANES)

    open_cell = (flags != 2).astype(F32)
    wall_x = shifted(open_cell[:1], "slab", -1)
    wall_y = shifted(open_cell[:, :1], "sub", -1)

    stride = 4 * cap + SUB
    send, slot = pl.pallas_call(
        functools.partial(splat_kernel, devices, cap),
        out_shape=(
            struct((devices * stride, LANES)),
            struct((blocks,), I32),
        ),
        in_specs=[vmem(), vmem(), vmem(), smem(), smem()],
        out_specs=(vmem(), smem()),
        scratch_shapes=[pltpu.SMEM((devices,), I32), pltpu.VMEM((8 * SUB, LANES), F32)],
        compiler_params=params(),
        name="splat",
    )(vel, weight, offset, owner[:, 0], brick[:, 0])

    exchange = functools.partial(
        lax.all_to_all, axis_name=("slab", "sub"), split_axis=0, concat_axis=0, tiled=True
    )
    arrived = exchange(send.reshape(devices, stride, LANES))
    arrived_brick = arrived[:, 4 * cap, :cap].astype(I32)
    count = jnp.sum((arrived_brick >= 0).astype(I32), axis=1)
    arrived_brick = arrived_brick.reshape(devices * cap)

    is_open = flags != 2
    next_x = jnp.concatenate([is_open[1:], wall_x > 0.0], 0)
    next_y = jnp.concatenate([is_open[:, 1:], wall_y > 0.0], 1)
    next_z = jnp.concatenate([is_open[:, :, 1:], jnp.zeros((span_x, span_y, 1), bool)], 2)
    code = (
        (is_open & next_x).astype(I32)
        + 2 * (is_open & next_y).astype(I32)
        + 4 * (is_open & next_z).astype(I32)
        + 8 * (flags == 1).astype(I32)
    ).reshape(grid4)

    whole = lambda *shape: pl.BlockSpec(shape, lambda x: (0,) * len(shape))
    one_layer = pl.BlockSpec((1, span_y, SUB, LANES), lambda x: (x, 0, 0, 0))
    three = pl.BlockSpec((3, 1, span_y, SUB, LANES), lambda x: (0, x, 0, 0, 0))
    g, r, div, edge_x, edge_y = pl.pallas_call(
        functools.partial(grid_kernel, devices, cap),
        grid=(span_x,),
        out_shape=(
            struct((3,) + grid4),
            struct((3,) + grid4),
            struct(grid4),
            struct((span_y, SUB, LANES)),
            struct((span_x, 1, SUB, LANES)),
        ),
        in_specs=[whole(devices * stride, LANES), smem(), smem(), one_layer],
        out_specs=(
            three,
            three,
            one_layer,
            whole(span_y, SUB, LANES),
            pl.BlockSpec((1, 1, SUB, LANES), lambda x: (x, 0, 0, 0)),
        ),
        scratch_shapes=[
            pltpu.VMEM((4, bricks, LANES), F32),
            pltpu.VMEM((span_y, SUB, LANES), F32),
            pltpu.VMEM((span_y + 1, SUB, LANES), F32),
        ],
        compiler_params=params(dimension_semantics=("arbitrary",)),
        name="grid",
    )(arrived.reshape(devices * stride, LANES), arrived_brick, count, code)

    padded = (span_x + 2, span_y + 2, SUB, LANES)
    p, reply = pl.pallas_call(
        functools.partial(solve_kernel, devices, cap),
        out_shape=(struct(padded), struct((devices * 3 * cap, LANES))),
        in_specs=[anywhere()] * 6 + [smem()],
        out_specs=(anywhere(), vmem()),
        scratch_shapes=[
            pltpu.VMEM((span_x + 1, span_y, SUB, LANES), F32),
            pltpu.VMEM((span_x, span_y + 1, SUB, LANES), F32),
            pltpu.VMEM(grid4, F32),
            pltpu.VMEM(grid4, F32),
            pltpu.VMEM(grid4, I32),
            pltpu.VMEM((3, bricks, LANES), F32),
            pltpu.VMEM((span_y, SUB, LANES), F32),
            pltpu.VMEM((span_x, SUB, LANES), F32),
            pltpu.VMEM(padded, F32),
            pltpu.VMEM(padded, F32),
            pltpu.VMEM(padded, F32),
            pltpu.SemaphoreType.DMA((6,)),
            pltpu.SemaphoreType.DMA,
            pltpu.SemaphoreType.DMA((16,)),
            pltpu.SemaphoreType.DMA((16,)),
        ],
        compiler_params=params(collective_id=0, has_side_effects=True),
        name="solve",
    )(g.reshape(3, bricks, LANES), r, div, code, edge_x, edge_y, arrived_brick)

    returned = exchange(reply.reshape(devices, 3 * cap, LANES))

    solved, pressure = pl.pallas_call(
        face_kernel,
        grid=(span_x,),
        out_shape=(struct((3,) + flags.shape), struct(flags.shape)),
        in_specs=[
            three,
            three,
            pl.BlockSpec((1, span_y + 2, SUB, LANES), lambda x: (x + 1, 0, 0, 0)),
            pl.BlockSpec((1, span_y + 2, SUB, LANES), lambda x: (x + 2, 0, 0, 0)),
        ],
        out_specs=(
            pl.BlockSpec((3, 1, span_y, span_z), lambda x: (0, x, 0, 0)),
            pl.BlockSpec((1, span_y, span_z), lambda x: (x, 0, 0)),
        ),
        scratch_shapes=[pltpu.VMEM((4, SUB * SUB, LANES), F32)],
        compiler_params=params(dimension_semantics=("arbitrary",)),
        cost_estimate=pl.CostEstimate(flops=10**7, bytes_accessed=24 * 10**6, transcendentals=0),
        name="faces",
    )(g, r, p, p)

    updated = pl.pallas_call(
        functools.partial(gather_kernel, cap),
        out_shape=struct((3, blocks, LANES)),
        in_specs=[vmem(), vmem(), smem(), vmem()],
        out_specs=vmem(),
        scratch_shapes=[pltpu.VMEM((3 * SUB, LANES), F32)],
        compiler_params=params(),
        name="gather",
    )(vel, offset, slot, returned.reshape(devices * 3 * cap, LANES))
    return updated.transpose(1, 0, 2), pressure, solved


def solution(mesh):
    in_specs = (
        P(("slab", "sub"), None, None),
        P(("slab", "sub"), None),
        P(("slab", "sub"), None),
        P(("slab", "sub"), None),
        P(("slab", "sub"), None),
        P("slab", "sub", None),
    )
    out_specs = (
        P(("slab", "sub"), None, None),
        P("slab", "sub", None),
        P(None, "slab", "sub", None),
    )
    return jax.shard_map(
        on_device, mesh=mesh, in_specs=in_specs, out_specs=out_specs, check_vma=False
    )
```

```python
import functools

import jax
import jax.numpy as jnp
from jax import lax
from jax.experimental import pallas as pl
from jax.experimental.pallas import tpu as pltpu
from jax.sharding import PartitionSpec as P

LANES = 128
SUB = 8
ITERS = 3

step_size = 0.15
MESH = pl.DeviceIdType.MESH
F32 = jnp.float32
I32 = jnp.int32
VMEM_LIMIT = 60 * 1024 * 1024


def vmem():
    return pl.BlockSpec(memory_space=pltpu.VMEM)


def smem():
    return pl.BlockSpec(memory_space=pltpu.SMEM)


def anywhere():
    return pl.BlockSpec(memory_space=pl.ANY)


def struct(shape, dtype=F32):
    return jax.ShapeDtypeStruct(shape, dtype)


def shifted(block, axis, distance):
    devices = range(lax.axis_size(axis))
    route = [(i - distance, i) for i in devices if i - distance in devices]
    return lax.ppermute(block, axis, route)


def splat_kernel(devices, cap, vel, wgt, off, owner, brick, send, slot, cnt, stage):
    @pl.loop(0, devices)
    def _(d):
        cnt[d] = 0

    stride = 4 * cap + SUB

    @pl.loop(0, devices)
    def _(d):
        tags = pl.multiple_of(d * stride + 4 * cap, SUB)
        send[pl.ds(tags, SUB), :] = jnp.full((SUB, LANES), -1.0, F32)

    lane = lax.broadcasted_iota(I32, (1, LANES), 1)
    cell = lax.broadcasted_iota(I32, (LANES, LANES), 0)

    @pl.loop(0, wgt.shape[0] // SUB)
    def _(group):
        base = pl.multiple_of(group * SUB, SUB)
        rows = pl.ds(base, SUB)
        w = wgt[rows, :]
        for c in range(4):
            value = w if c == 3 else vel[c, rows, :] * w
            high = value.astype(jnp.bfloat16).astype(F32)
            stage[c * SUB : (c + 1) * SUB, :] = high
            stage[(c + 4) * SUB : (c + 5) * SUB, :] = value - high
        for j in range(SUB):
            lhs = stage[pl.ds(j, SUB, stride=SUB), :].astype(jnp.bfloat16)
            where = off[pl.ds(base + j, 1), :]
            hit = (cell == where).astype(F32).astype(jnp.bfloat16)
            sums = lax.dot_general(
                lhs, hit, (((1,), (1,)), ((), ())), preferred_element_type=F32
            )
            sums = sums[0:4] + sums[4:8]
            o = owner[base + j]
            r = cnt[o]
            cnt[o] = r + 1
            tags = pl.ds(o * stride + 4 * cap, 1)
            send[tags, :] = jnp.where(lane == r, brick[base + j].astype(F32), send[tags, :])
            slot[base + j] = o * (3 * cap) + r
            for c in range(4):
                send[pl.ds(o * stride + c * cap + r, 1), :] = sums[c : c + 1]


def grid_kernel(devices, cap, arrived, brick, count, code, g_out, r_out, d_out, ex, ey, tot, prev, uy):
    x = pl.program_id(0)
    span_y = code.shape[1]
    chunk = SUB

    @pl.when(x == 0)
    def _():
        piece = 128

        @pl.loop(0, tot.shape[1] // piece)
        def _(i):
            for c in range(4):
                tot[c, pl.ds(pl.multiple_of(i * piece, piece), piece), :] = jnp.zeros((piece, LANES), F32)

        prev[...] = jnp.zeros_like(prev)
        uy[0] = jnp.zeros((SUB, LANES), F32)

        @pl.loop(0, devices)
        def _(d):
            used = count[d]

            @pl.loop(0, lax.div(used + 1, 2))
            def _(pair):
                s = 2 * pair
                second = s + 1 < used
                b = brick[d * cap + s]
                b_second = jnp.where(second, brick[d * cap + s + 1], b)
                same = b_second == b
                for c in range(4):
                    row = d * (4 * cap + SUB) + c * cap + s
                    held = tot[c, pl.ds(b, 1), :] + arrived[pl.ds(row, 1), :]
                    other = jnp.where(same, held, tot[c, pl.ds(b_second, 1), :])
                    added = jnp.where(second, arrived[pl.ds(row + 1, 1), :], 0.0)
                    tot[c, pl.ds(b, 1), :] = held
                    tot[c, pl.ds(b_second, 1), :] = other + added

    lane = lax.broadcasted_iota(I32, (chunk, SUB, LANES), 2)

    @pl.loop(0, span_y // chunk)
    def _(k):
        y = k * chunk
        rows = pl.ds(pl.multiple_of((x * span_y + y) * SUB, SUB), chunk * SUB)
        strips = pl.ds(y, chunk)
        kind = code[0, strips]
        inverse = 1.0 / (tot[3, rows, :].reshape(chunk, SUB, LANES) + 1.0)
        moved = []
        for a in range(3):
            face = ((kind >> a) & 1).astype(F32)
            guess = tot[a, rows, :].reshape(chunk, SUB, LANES) * inverse
            g_out[a, 0, strips] = guess
            r_out[a, 0, strips] = face * inverse
            moved.append(face * guess)
        ux, v, uz = moved
        uy[pl.ds(y + 1, chunk)] = v
        turned = pltpu.roll(uz, 1, 2)
        before = jnp.where(lane == 0, pltpu.roll(turned, 1, 1), turned)
        spread = ux - prev[strips]
        spread = spread + (v - uy[strips])
        spread = spread + (uz - before)
        d_out[0, strips] = spread
        prev[strips] = ux

    ey[0, 0] = uy[span_y]
    ex[...] = prev[...]


def solve_kernel(
    devices, cap, g_hbm, r_hbm, d_hbm, k_hbm, ex_hbm, ey_hbm, brick, p_out, reply,
    rx, ry, rz, div, kind, g, hx, hy, p1, p2, p3, here, out_sem, send_sem, recv_sem,
):
    span_x, span_y = div.shape[0], div.shape[1]
    chunk = SUB
    n_slab, n_sub = lax.axis_size("slab"), lax.axis_size("sub")
    slab, sub = lax.axis_index("slab"), lax.axis_index("sub")
    east, west = lax.rem(slab + 1, n_slab), lax.rem(slab + n_slab - 1, n_slab)
    north, south = lax.rem(sub + 1, n_sub), lax.rem(sub + n_sub - 1, n_sub)
    locals_ = [
        pltpu.make_async_copy(src, dst, here.at[i])
        for i, (src, dst) in enumerate(
            [
                (d_hbm, div),
                (k_hbm, kind),
                (r_hbm.at[0], rx.at[pl.ds(1, span_x)]),
                (r_hbm.at[1], ry.at[:, pl.ds(1, span_y)]),
                (r_hbm.at[2], rz),
                (g_hbm, g),
            ]
        )
    ]
    for copy in locals_:
        copy.start()
    barrier = pltpu.get_barrier_semaphore()
    for axis, peer in (("slab", east), ("slab", west), ("sub", north), ("sub", south)):
        pl.semaphore_signal(barrier, inc=1, device_id={axis: peer}, device_id_type=MESH)
    pl.semaphore_wait(barrier, 4)

    def remote(index, src, dst, axis, up):
        place, size = (slab, n_slab) if axis == "slab" else (sub, n_sub)
        after, before = place < size - 1, place > 0
        peer = {"slab": (east, west), "sub": (north, south)}[axis][0 if up else 1]
        copy = pltpu.make_async_remote_copy(
            src_ref=src, dst_ref=dst, send_sem=send_sem.at[index], recv_sem=recv_sem.at[index],
            device_id={axis: peer}, device_id_type=MESH,
        )
        return copy, (after if up else before), (before if up else after)

    def begin(*moves):
        for copy, sends, _ in moves:
            pl.when(sends)(copy.start)

    def finish(*moves):
        for copy, sends, gets in moves:
            pl.when(sends)(copy.wait_send)
            pl.when(gets)(copy.wait_recv)

    xs, ys = pl.ds(1, span_x), pl.ds(1, span_y)
    flow_x = remote(0, ex_hbm, hx, "slab", True)
    flow_y = remote(1, ey_hbm.at[:, 0], hy, "sub", True)
    link_x = remote(2, r_hbm.at[0, span_x - 1], rx.at[0], "slab", True)
    link_y = remote(3, r_hbm.at[1, :, span_y - 1], ry.at[:, 0], "sub", True)
    begin(flow_y, flow_x)

    def halos(field, first):
        return (
            remote(first, field.at[1, ys], field.at[span_x + 1, ys], "slab", False),
            remote(first + 1, field.at[span_x, ys], field.at[0, ys], "slab", True),
            remote(first + 2, field.at[xs, 1], field.at[xs, span_y + 1], "sub", False),
            remote(first + 3, field.at[xs, span_y], field.at[xs, 0], "sub", True),
        )

    nothing = jnp.zeros((SUB, LANES), F32)

    @pl.when(slab == 0)
    def _():
        @pl.loop(0, span_y)
        def _(y):
            hx[y] = nothing
            rx[0, y] = nothing
            for field in (p1, p2):
                field[0, y + 1] = nothing

    @pl.when(slab == n_slab - 1)
    def _():
        @pl.loop(0, span_y)
        def _(y):
            for field in (p1, p2, p3):
                field[span_x + 1, y + 1] = nothing

    @pl.when(sub == 0)
    def _():
        @pl.loop(0, span_x)
        def _(x):
            hy[x] = nothing
            ry[x, 0] = nothing
            for field in (p1, p2):
                field[x + 1, 0] = nothing

    @pl.when(sub == n_sub - 1)
    def _():
        @pl.loop(0, span_x)
        def _(x):
            for field in (p1, p2, p3):
                field[x + 1, span_y + 1] = nothing

    lane = lax.broadcasted_iota(I32, (chunk, SUB, LANES), 2)

    def onward(value):
        turned = pltpu.roll(value, LANES - 1, 2)
        return jnp.where(lane == LANES - 1, pltpu.roll(turned, SUB - 1, 1), turned)

    def back(value):
        turned = pltpu.roll(value, 1, 2)
        return jnp.where(lane == 0, pltpu.roll(turned, 1, 1), turned)

    def layers(low, high, body):
        @pl.loop(low, high)
        def _(x):
            @pl.loop(0, span_y // chunk)
            def _(k):
                body(x, k * chunk)

    def lifted(x, y, raised):
        wet = kind[x, pl.ds(y, chunk)] >= 8
        return jnp.where(wet, jnp.maximum(raised, 0.0), 0.0)

    def start(x, y):
        p1[x + 1, pl.ds(y + 1, chunk)] = lifted(x, y, -step_size * div[x, pl.ds(y, chunk)])

    for i in (0, 1):
        locals_[i].wait()
    finish(flow_y)

    @pl.loop(0, span_x)
    def _(x):
        div[x, 0] = div[x, 0] - hy[x]

    down, up, south_1, north_1 = halos(p1, 4)
    layers(span_x - 1, span_x, start)
    begin(up, link_x, link_y)
    layers(1, span_x - 1, start)
    finish(flow_x)

    @pl.loop(0, span_y)
    def _(y):
        div[0, y] = div[0, y] - hx[y]

    layers(0, 1, start)
    begin(down, south_1, north_1)
    for i in (2, 3, 4):
        locals_[i].wait()

    def ascend(old, new):
        def body(x, y):
            strips, inner = pl.ds(y, chunk), pl.ds(y + 1, chunk)
            p = old[x + 1, inner]
            flow = rz[x, strips] * (p - onward(p))
            spread = div[x, strips] + (flow - back(flow))
            spread = spread + rx[x + 1, strips] * (p - old[x + 2, inner])
            spread = spread - rx[x, strips] * (old[x, inner] - p)
            spread = spread + ry[x, inner] * (p - old[x + 1, pl.ds(y + 2, chunk)])
            spread = spread - ry[x, strips] * (old[x + 1, strips] - p)
            new[x + 1, inner] = lifted(x, y, p - step_size * spread)

        return body

    body = ascend(p1, p2)
    down_2, up_2, south_2, north_2 = halos(p2, 8)
    finish(link_y, south_1, north_1)
    layers(1, span_x - 1, body)
    finish(link_x, up, down)
    layers(0, 1, body)
    begin(down_2)
    layers(span_x - 1, span_x, body)
    begin(up_2, south_2, north_2)

    body = ascend(p2, p3)
    down_3, _, south_3, _ = halos(p3, 12)
    finish(south_2, north_2)
    layers(1, span_x - 1, body)
    finish(up_2, down_2)
    layers(0, 1, body)
    begin(down_3)
    layers(span_x - 1, span_x, body)
    begin(south_3)
    locals_[5].wait()

    def settle(x, y):
        strips, inner = pl.ds(y, chunk), pl.ds(y + 1, chunk)
        rows = pl.ds(pl.multiple_of((x * span_y + y) * SUB, SUB), chunk * SUB)
        p = p3[x + 1, inner]
        after = (p3[x + 2, inner], p3[x + 1, pl.ds(y + 2, chunk)], onward(p))
        link = (rx[x + 1, strips], ry[x, inner], rz[x, strips])
        for a in range(3):
            shut = jnp.where(link[a] > 0.0, 0.0, -g[a, rows, :].reshape(chunk, SUB, LANES))
            change = shut + link[a] * (p - after[a])
            g[a, rows, :] = change.reshape(chunk * SUB, LANES)

    finish(south_3)
    layers(0, span_x - 1, settle)
    finish(down_3)
    leave = pltpu.make_async_copy(p3, p_out, out_sem)
    leave.start()
    layers(span_x - 1, span_x, settle)

    @pl.loop(0, devices)
    def _(d):
        @pl.loop(0, cap, unroll=8)
        def _(s):
            b = jnp.maximum(brick[d * cap + s], 0)
            for a in range(3):
                reply[pl.ds(d * (3 * cap) + a * cap + s, 1), :] = g[a, pl.ds(b, 1), :]

    leave.wait()


def face_kernel(g, r, p_here, p_next, u_out, p_out, stage):
    span_y = g.shape[2]
    lane = lax.broadcasted_iota(I32, (SUB, SUB, LANES), 2)

    @pl.loop(0, span_y // SUB)
    def _(k):
        y = pl.multiple_of(k * SUB, SUB)
        strips, inner = pl.ds(y, SUB), pl.ds(y + 1, SUB)
        p = p_here[0, inner]
        turned = pltpu.roll(p, LANES - 1, 2)
        up = jnp.where(lane == LANES - 1, pltpu.roll(turned, SUB - 1, 1), turned)
        after = (p_next[0, inner], p_here[0, pl.ds(y + 2, SUB)], up)
        stage[3] = p.reshape(SUB * SUB, LANES)
        for a in range(3):
            link = r[a, 0, strips]
            face = jnp.where(link > 0.0, g[a, 0, strips] + link * (p - after[a]), 0.0)
            stage[a] = face.reshape(SUB * SUB, LANES)
        for z in range(SUB):
            cols = slice(z * LANES, (z + 1) * LANES)
            pick = pl.ds(z, SUB, stride=SUB)
            p_out[0, strips, cols] = stage[3, pick, :]
            for a in range(3):
                u_out[a, 0, strips, cols] = stage[a, pick, :]


def gather_kernel(cap, vel, off, slot, back, out, stage):
    @pl.loop(0, off.shape[0] // SUB)
    def _(group):
        base = pl.multiple_of(group * SUB, SUB)
        rows = pl.ds(base, SUB)
        for j in range(SUB):
            s = slot[base + j]
            for c in range(3):
                stage[pl.ds(c * SUB + j, 1), :] = back[pl.ds(s + c * cap, 1), :]
        where = off[rows, :]
        for c in range(3):
            picked = jnp.take_along_axis(
                stage[c * SUB : (c + 1) * SUB, :], where, axis=1, mode="promise_in_bounds"
            )
            out[c, rows, :] = vel[c, rows, :] + picked


def on_device(velocity, weight, offset, owner, brick, flags):
    devices = lax.axis_size("slab") * lax.axis_size("sub")
    blocks = velocity.shape[0]
    cap = 2 * blocks // devices
    span_x, span_y, span_z = flags.shape
    bricks = span_x * span_y * span_z // LANES
    params = functools.partial(pltpu.CompilerParams, vmem_limit_bytes=VMEM_LIMIT)
    vel = velocity.transpose(1, 0, 2)
    grid4 = (span_x, span_y, SUB, LANES)

    open_cell = (flags != 2).astype(F32)
    wall_x = shifted(open_cell[:1], "slab", -1)
    wall_y = shifted(open_cell[:, :1], "sub", -1)

    stride = 4 * cap + SUB
    send, slot = pl.pallas_call(
        functools.partial(splat_kernel, devices, cap),
        out_shape=(
            struct((devices * stride, LANES)),
            struct((blocks,), I32),
        ),
        in_specs=[vmem(), vmem(), vmem(), smem(), smem()],
        out_specs=(vmem(), smem()),
        scratch_shapes=[pltpu.SMEM((devices,), I32), pltpu.VMEM((8 * SUB, LANES), F32)],
        compiler_params=params(),
        name="splat",
    )(vel, weight, offset, owner[:, 0], brick[:, 0])

    exchange = functools.partial(
        lax.all_to_all, axis_name=("slab", "sub"), split_axis=0, concat_axis=0, tiled=True
    )
    arrived = exchange(send.reshape(devices, stride, LANES))
    arrived_brick = arrived[:, 4 * cap, :cap].astype(I32)
    count = jnp.sum((arrived_brick >= 0).astype(I32), axis=1)
    arrived_brick = arrived_brick.reshape(devices * cap)

    is_open = flags != 2
    next_x = jnp.concatenate([is_open[1:], wall_x > 0.0], 0)
    next_y = jnp.concatenate([is_open[:, 1:], wall_y > 0.0], 1)
    next_z = jnp.concatenate([is_open[:, :, 1:], jnp.zeros((span_x, span_y, 1), bool)], 2)
    code = (
        (is_open & next_x).astype(I32)
        + 2 * (is_open & next_y).astype(I32)
        + 4 * (is_open & next_z).astype(I32)
        + 8 * (flags == 1).astype(I32)
    ).reshape(grid4)

    whole = lambda *shape: pl.BlockSpec(shape, lambda x: (0,) * len(shape))
    one_layer = pl.BlockSpec((1, span_y, SUB, LANES), lambda x: (x, 0, 0, 0))
    three = pl.BlockSpec((3, 1, span_y, SUB, LANES), lambda x: (0, x, 0, 0, 0))
    g, r, div, edge_x, edge_y = pl.pallas_call(
        functools.partial(grid_kernel, devices, cap),
        grid=(span_x,),
        out_shape=(
            struct((3,) + grid4),
            struct((3,) + grid4),
            struct(grid4),
            struct((span_y, SUB, LANES)),
            struct((span_x, 1, SUB, LANES)),
        ),
        in_specs=[whole(devices * stride, LANES), smem(), smem(), one_layer],
        out_specs=(
            three,
            three,
            one_layer,
            whole(span_y, SUB, LANES),
            pl.BlockSpec((1, 1, SUB, LANES), lambda x: (x, 0, 0, 0)),
        ),
        scratch_shapes=[
            pltpu.VMEM((4, bricks, LANES), F32),
            pltpu.VMEM((span_y, SUB, LANES), F32),
            pltpu.VMEM((span_y + 1, SUB, LANES), F32),
        ],
        compiler_params=params(dimension_semantics=("arbitrary",)),
        name="grid",
    )(arrived.reshape(devices * stride, LANES), arrived_brick, count, code)

    padded = (span_x + 2, span_y + 2, SUB, LANES)
    p, reply = pl.pallas_call(
        functools.partial(solve_kernel, devices, cap),
        out_shape=(struct(padded), struct((devices * 3 * cap, LANES))),
        in_specs=[anywhere()] * 6 + [smem()],
        out_specs=(anywhere(), vmem()),
        scratch_shapes=[
            pltpu.VMEM((span_x + 1, span_y, SUB, LANES), F32),
            pltpu.VMEM((span_x, span_y + 1, SUB, LANES), F32),
            pltpu.VMEM(grid4, F32),
            pltpu.VMEM(grid4, F32),
            pltpu.VMEM(grid4, I32),
            pltpu.VMEM((3, bricks, LANES), F32),
            pltpu.VMEM((span_y, SUB, LANES), F32),
            pltpu.VMEM((span_x, SUB, LANES), F32),
            pltpu.VMEM(padded, F32),
            pltpu.VMEM(padded, F32),
            pltpu.VMEM(padded, F32),
            pltpu.SemaphoreType.DMA((6,)),
            pltpu.SemaphoreType.DMA,
            pltpu.SemaphoreType.DMA((16,)),
            pltpu.SemaphoreType.DMA((16,)),
        ],
        compiler_params=params(collective_id=0, has_side_effects=True),
        name="solve",
    )(g.reshape(3, bricks, LANES), r, div, code, edge_x, edge_y, arrived_brick)

    returned = exchange(reply.reshape(devices, 3 * cap, LANES))

    solved, pressure = pl.pallas_call(
        face_kernel,
        grid=(span_x,),
        out_shape=(struct((3,) + flags.shape), struct(flags.shape)),
        in_specs=[
            three,
            three,
            pl.BlockSpec((1, span_y + 2, SUB, LANES), lambda x: (x + 1, 0, 0, 0)),
            pl.BlockSpec((1, span_y + 2, SUB, LANES), lambda x: (x + 2, 0, 0, 0)),
        ],
        out_specs=(
            pl.BlockSpec((3, 1, span_y, span_z), lambda x: (0, x, 0, 0)),
            pl.BlockSpec((1, span_y, span_z), lambda x: (x, 0, 0)),
        ),
        scratch_shapes=[pltpu.VMEM((4, SUB * SUB, LANES), F32)],
        compiler_params=params(dimension_semantics=("arbitrary",)),
        cost_estimate=pl.CostEstimate(flops=10**7, bytes_accessed=24 * 10**6, transcendentals=0),
        name="faces",
    )(g, r, p, p)

    updated = pl.pallas_call(
        functools.partial(gather_kernel, cap),
        out_shape=struct((3, blocks, LANES)),
        in_specs=[vmem(), vmem(), smem(), vmem()],
        out_specs=vmem(),
        scratch_shapes=[pltpu.VMEM((3 * SUB, LANES), F32)],
        compiler_params=params(),
        name="gather",
    )(vel, offset, slot, returned.reshape(devices * 3 * cap, LANES))
    return updated.transpose(1, 0, 2), pressure, solved


def solution(mesh):
    in_specs = (
        P(("slab", "sub"), None, None),
        P(("slab", "sub"), None),
        P(("slab", "sub"), None),
        P(("slab", "sub"), None),
        P(("slab", "sub"), None),
        P("slab", "sub", None),
    )
    out_specs = (
        P(("slab", "sub"), None, None),
        P("slab", "sub", None),
        P(None, "slab", "sub", None),
    )
    return jax.shard_map(
        on_device, mesh=mesh, in_specs=in_specs, out_specs=out_specs, check_vma=False
    )
```

```python
import functools

import jax
import jax.numpy as jnp
from jax import lax
from jax.experimental import pallas as pl
from jax.experimental.pallas import tpu as pltpu
from jax.sharding import PartitionSpec as P

LANES = 128
SUB = 8
ITERS = 3

step_size = 0.15
MESH = pl.DeviceIdType.MESH
F32 = jnp.float32
I32 = jnp.int32
VMEM_LIMIT = 60 * 1024 * 1024


def vmem():
    return pl.BlockSpec(memory_space=pltpu.VMEM)


def smem():
    return pl.BlockSpec(memory_space=pltpu.SMEM)


def anywhere():
    return pl.BlockSpec(memory_space=pl.ANY)


def struct(shape, dtype=F32):
    return jax.ShapeDtypeStruct(shape, dtype)


def shifted(block, axis, distance):
    devices = range(lax.axis_size(axis))
    route = [(i - distance, i) for i in devices if i - distance in devices]
    return lax.ppermute(block, axis, route)


def splat_kernel(devices, cap, vel, wgt, off, owner, brick, send, slot, cnt, stage):
    @pl.loop(0, devices)
    def _(d):
        cnt[d] = 0

    stride = 4 * cap + SUB

    @pl.loop(0, devices)
    def _(d):
        tags = pl.multiple_of(d * stride + 4 * cap, SUB)
        send[pl.ds(tags, SUB), :] = jnp.full((SUB, LANES), -1.0, F32)

    lane = lax.broadcasted_iota(I32, (1, LANES), 1)
    cell = lax.broadcasted_iota(I32, (LANES, LANES), 0)

    @pl.loop(0, wgt.shape[0] // SUB, unroll=2)
    def _(group):
        base = pl.multiple_of(group * SUB, SUB)
        rows = pl.ds(base, SUB)
        w = wgt[rows, :]
        for c in range(4):
            value = w if c == 3 else vel[c, rows, :] * w
            high = value.astype(jnp.bfloat16).astype(F32)
            stage[c * SUB : (c + 1) * SUB, :] = high
            stage[(c + 4) * SUB : (c + 5) * SUB, :] = value - high
        for j in range(SUB):
            lhs = stage[pl.ds(j, SUB, stride=SUB), :].astype(jnp.bfloat16)
            where = off[pl.ds(base + j, 1), :]
            hit = (cell == where).astype(F32).astype(jnp.bfloat16)
            sums = lax.dot_general(
                lhs, hit, (((1,), (1,)), ((), ())), preferred_element_type=F32
            )
            sums = sums[0:4] + sums[4:8]
            o = owner[base + j]
            r = cnt[o]
            cnt[o] = r + 1
            tags = pl.ds(o * stride + 4 * cap, 1)
            send[tags, :] = jnp.where(lane == r, brick[base + j].astype(F32), send[tags, :])
            slot[base + j] = o * (3 * cap) + r
            for c in range(4):
                send[pl.ds(o * stride + c * cap + r, 1), :] = sums[c : c + 1]


def grid_kernel(devices, cap, arrived, brick, count, code, g_out, r_out, d_out, ex, ey, tot, prev, uy):
    x = pl.program_id(0)
    span_y = code.shape[1]
    chunk = SUB

    @pl.when(x == 0)
    def _():
        piece = 128

        @pl.loop(0, tot.shape[1] // piece)
        def _(i):
            for c in range(4):
                tot[c, pl.ds(pl.multiple_of(i * piece, piece), piece), :] = jnp.zeros((piece, LANES), F32)

        prev[...] = jnp.zeros_like(prev)
        uy[0] = jnp.zeros((SUB, LANES), F32)

        @pl.loop(0, devices)
        def _(d):
            used = count[d]

            @pl.loop(0, lax.div(used + 1, 2))
            def _(pair):
                s = 2 * pair
                second = s + 1 < used
                b = brick[d * cap + s]
                b_second = jnp.where(second, brick[d * cap + s + 1], b)
                same = b_second == b
                for c in range(4):
                    row = d * (4 * cap + SUB) + c * cap + s
                    held = tot[c, pl.ds(b, 1), :] + arrived[pl.ds(row, 1), :]
                    other = jnp.where(same, held, tot[c, pl.ds(b_second, 1), :])
                    added = jnp.where(second, arrived[pl.ds(row + 1, 1), :], 0.0)
                    tot[c, pl.ds(b, 1), :] = held
                    tot[c, pl.ds(b_second, 1), :] = other + added

    lane = lax.broadcasted_iota(I32, (chunk, SUB, LANES), 2)

    @pl.loop(0, span_y // chunk, unroll=2)
    def _(k):
        y = k * chunk
        rows = pl.ds(pl.multiple_of((x * span_y + y) * SUB, SUB), chunk * SUB)
        strips = pl.ds(y, chunk)
        kind = code[0, strips]
        inverse = 1.0 / (tot[3, rows, :].reshape(chunk, SUB, LANES) + 1.0)
        moved = []
        for a in range(3):
            face = ((kind >> a) & 1).astype(F32)
            guess = tot[a, rows, :].reshape(chunk, SUB, LANES) * inverse
            g_out[a, 0, strips] = guess
            r_out[a, 0, strips] = face * inverse
            moved.append(face * guess)
        ux, v, uz = moved
        uy[pl.ds(y + 1, chunk)] = v
        turned = pltpu.roll(uz, 1, 2)
        before = jnp.where(lane == 0, pltpu.roll(turned, 1, 1), turned)
        spread = ux - prev[strips]
        spread = spread + (v - uy[strips])
        spread = spread + (uz - before)
        d_out[0, strips] = spread
        prev[strips] = ux

    ey[0, 0] = uy[span_y]
    ex[...] = prev[...]


def solve_kernel(
    devices, cap, g_hbm, r_hbm, d_hbm, k_hbm, ex_hbm, ey_hbm, brick, p_out, reply,
    rx, ry, rz, div, kind, g, hx, hy, p1, p2, p3, here, out_sem, send_sem, recv_sem,
):
    span_x, span_y = div.shape[0], div.shape[1]
    chunk = SUB
    n_slab, n_sub = lax.axis_size("slab"), lax.axis_size("sub")
    slab, sub = lax.axis_index("slab"), lax.axis_index("sub")
    east, west = lax.rem(slab + 1, n_slab), lax.rem(slab + n_slab - 1, n_slab)
    north, south = lax.rem(sub + 1, n_sub), lax.rem(sub + n_sub - 1, n_sub)
    locals_ = [
        pltpu.make_async_copy(src, dst, here.at[i])
        for i, (src, dst) in enumerate(
            [
                (d_hbm, div),
                (k_hbm, kind),
                (r_hbm.at[0], rx.at[pl.ds(1, span_x)]),
                (r_hbm.at[1], ry.at[:, pl.ds(1, span_y)]),
                (r_hbm.at[2], rz),
                (g_hbm, g),
            ]
        )
    ]
    for copy in locals_:
        copy.start()
    barrier = pltpu.get_barrier_semaphore()
    for axis, peer in (("slab", east), ("slab", west), ("sub", north), ("sub", south)):
        pl.semaphore_signal(barrier, inc=1, device_id={axis: peer}, device_id_type=MESH)
    pl.semaphore_wait(barrier, 4)

    def remote(index, src, dst, axis, up):
        place, size = (slab, n_slab) if axis == "slab" else (sub, n_sub)
        after, before = place < size - 1, place > 0
        peer = {"slab": (east, west), "sub": (north, south)}[axis][0 if up else 1]
        copy = pltpu.make_async_remote_copy(
            src_ref=src, dst_ref=dst, send_sem=send_sem.at[index], recv_sem=recv_sem.at[index],
            device_id={axis: peer}, device_id_type=MESH,
        )
        return copy, (after if up else before), (before if up else after)

    def begin(*moves):
        for copy, sends, _ in moves:
            pl.when(sends)(copy.start)

    def finish(*moves):
        for copy, sends, gets in moves:
            pl.when(sends)(copy.wait_send)
            pl.when(gets)(copy.wait_recv)

    xs, ys = pl.ds(1, span_x), pl.ds(1, span_y)
    flow_x = remote(0, ex_hbm, hx, "slab", True)
    flow_y = remote(1, ey_hbm.at[:, 0], hy, "sub", True)
    link_x = remote(2, r_hbm.at[0, span_x - 1], rx.at[0], "slab", True)
    link_y = remote(3, r_hbm.at[1, :, span_y - 1], ry.at[:, 0], "sub", True)
    begin(flow_y, flow_x)

    def halos(field, first):
        return (
            remote(first, field.at[1, ys], field.at[span_x + 1, ys], "slab", False),
            remote(first + 1, field.at[span_x, ys], field.at[0, ys], "slab", True),
            remote(first + 2, field.at[xs, 1], field.at[xs, span_y + 1], "sub", False),
            remote(first + 3, field.at[xs, span_y], field.at[xs, 0], "sub", True),
        )

    nothing = jnp.zeros((SUB, LANES), F32)

    @pl.when(slab == 0)
    def _():
        @pl.loop(0, span_y)
        def _(y):
            hx[y] = nothing
            rx[0, y] = nothing
            for field in (p1, p2):
                field[0, y + 1] = nothing

    @pl.when(slab == n_slab - 1)
    def _():
        @pl.loop(0, span_y)
        def _(y):
            for field in (p1, p2, p3):
                field[span_x + 1, y + 1] = nothing

    @pl.when(sub == 0)
    def _():
        @pl.loop(0, span_x)
        def _(x):
            hy[x] = nothing
            ry[x, 0] = nothing
            for field in (p1, p2):
                field[x + 1, 0] = nothing

    @pl.when(sub == n_sub - 1)
    def _():
        @pl.loop(0, span_x)
        def _(x):
            for field in (p1, p2, p3):
                field[x + 1, span_y + 1] = nothing

    lane = lax.broadcasted_iota(I32, (chunk, SUB, LANES), 2)

    def onward(value):
        turned = pltpu.roll(value, LANES - 1, 2)
        return jnp.where(lane == LANES - 1, pltpu.roll(turned, SUB - 1, 1), turned)

    def back(value):
        turned = pltpu.roll(value, 1, 2)
        return jnp.where(lane == 0, pltpu.roll(turned, 1, 1), turned)

    def layers(low, high, body):
        @pl.loop(low, high)
        def _(x):
            @pl.loop(0, span_y // chunk, unroll=2)
            def _(k):
                body(x, k * chunk)

    def lifted(x, y, raised):
        wet = kind[x, pl.ds(y, chunk)] >= 8
        return jnp.where(wet, jnp.maximum(raised, 0.0), 0.0)

    def start(x, y):
        p1[x + 1, pl.ds(y + 1, chunk)] = lifted(x, y, -step_size * div[x, pl.ds(y, chunk)])

    for i in (0, 1):
        locals_[i].wait()
    finish(flow_y)

    @pl.loop(0, span_x)
    def _(x):
        div[x, 0] = div[x, 0] - hy[x]

    down, up, south_1, north_1 = halos(p1, 4)
    layers(span_x - 1, span_x, start)
    begin(up, link_x, link_y)
    layers(1, span_x - 1, start)
    finish(flow_x)

    @pl.loop(0, span_y)
    def _(y):
        div[0, y] = div[0, y] - hx[y]

    layers(0, 1, start)
    begin(down, south_1, north_1)
    for i in (2, 3, 4):
        locals_[i].wait()

    def ascend(old, new):
        def body(x, y):
            strips, inner = pl.ds(y, chunk), pl.ds(y + 1, chunk)
            p = old[x + 1, inner]
            flow = rz[x, strips] * (p - onward(p))
            spread = div[x, strips] + (flow - back(flow))
            spread = spread + rx[x + 1, strips] * (p - old[x + 2, inner])
            spread = spread - rx[x, strips] * (old[x, inner] - p)
            spread = spread + ry[x, inner] * (p - old[x + 1, pl.ds(y + 2, chunk)])
            spread = spread - ry[x, strips] * (old[x + 1, strips] - p)
            new[x + 1, inner] = lifted(x, y, p - step_size * spread)

        return body

    body = ascend(p1, p2)
    down_2, up_2, south_2, north_2 = halos(p2, 8)
    finish(link_y, south_1, north_1)
    layers(1, span_x - 1, body)
    finish(link_x, up, down)
    layers(0, 1, body)
    begin(down_2)
    layers(span_x - 1, span_x, body)
    begin(up_2, south_2, north_2)

    body = ascend(p2, p3)
    down_3, _, south_3, _ = halos(p3, 12)
    finish(south_2, north_2)
    layers(1, span_x - 1, body)
    finish(up_2, down_2)
    layers(0, 1, body)
    begin(down_3)
    layers(span_x - 1, span_x, body)
    begin(south_3)
    locals_[5].wait()

    def settle(x, y):
        strips, inner = pl.ds(y, chunk), pl.ds(y + 1, chunk)
        rows = pl.ds(pl.multiple_of((x * span_y + y) * SUB, SUB), chunk * SUB)
        p = p3[x + 1, inner]
        after = (p3[x + 2, inner], p3[x + 1, pl.ds(y + 2, chunk)], onward(p))
        link = (rx[x + 1, strips], ry[x, inner], rz[x, strips])
        for a in range(3):
            shut = jnp.where(link[a] > 0.0, 0.0, -g[a, rows, :].reshape(chunk, SUB, LANES))
            change = shut + link[a] * (p - after[a])
            g[a, rows, :] = change.reshape(chunk * SUB, LANES)

    finish(south_3)
    layers(0, span_x - 1, settle)
    finish(down_3)
    leave = pltpu.make_async_copy(p3, p_out, out_sem)
    leave.start()
    layers(span_x - 1, span_x, settle)

    @pl.loop(0, devices)
    def _(d):
        @pl.loop(0, cap, unroll=8)
        def _(s):
            b = jnp.maximum(brick[d * cap + s], 0)
            for a in range(3):
                reply[pl.ds(d * (3 * cap) + a * cap + s, 1), :] = g[a, pl.ds(b, 1), :]

    leave.wait()


def face_kernel(g, r, p_here, p_next, u_out, p_out, stage):
    span_y = g.shape[2]
    lane = lax.broadcasted_iota(I32, (SUB, SUB, LANES), 2)

    @pl.loop(0, span_y // SUB)
    def _(k):
        y = pl.multiple_of(k * SUB, SUB)
        strips, inner = pl.ds(y, SUB), pl.ds(y + 1, SUB)
        p = p_here[0, inner]
        turned = pltpu.roll(p, LANES - 1, 2)
        up = jnp.where(lane == LANES - 1, pltpu.roll(turned, SUB - 1, 1), turned)
        after = (p_next[0, inner], p_here[0, pl.ds(y + 2, SUB)], up)
        stage[3] = p.reshape(SUB * SUB, LANES)
        for a in range(3):
            link = r[a, 0, strips]
            face = jnp.where(link > 0.0, g[a, 0, strips] + link * (p - after[a]), 0.0)
            stage[a] = face.reshape(SUB * SUB, LANES)
        for z in range(SUB):
            cols = slice(z * LANES, (z + 1) * LANES)
            pick = pl.ds(z, SUB, stride=SUB)
            p_out[0, strips, cols] = stage[3, pick, :]
            for a in range(3):
                u_out[a, 0, strips, cols] = stage[a, pick, :]


def gather_kernel(cap, vel, off, slot, back, out, stage):
    @pl.loop(0, off.shape[0] // SUB, unroll=4)
    def _(group):
        base = pl.multiple_of(group * SUB, SUB)
        rows = pl.ds(base, SUB)
        for j in range(SUB):
            s = slot[base + j]
            for c in range(3):
                stage[pl.ds(c * SUB + j, 1), :] = back[pl.ds(s + c * cap, 1), :]
        where = off[rows, :]
        for c in range(3):
            picked = jnp.take_along_axis(
                stage[c * SUB : (c + 1) * SUB, :], where, axis=1, mode="promise_in_bounds"
            )
            out[c, rows, :] = vel[c, rows, :] + picked


def on_device(velocity, weight, offset, owner, brick, flags):
    devices = lax.axis_size("slab") * lax.axis_size("sub")
    blocks = velocity.shape[0]
    cap = 2 * blocks // devices
    span_x, span_y, span_z = flags.shape
    bricks = span_x * span_y * span_z // LANES
    params = functools.partial(pltpu.CompilerParams, vmem_limit_bytes=VMEM_LIMIT)
    vel = velocity.transpose(1, 0, 2)
    grid4 = (span_x, span_y, SUB, LANES)

    open_cell = (flags != 2).astype(F32)
    wall_x = shifted(open_cell[:1], "slab", -1)
    wall_y = shifted(open_cell[:, :1], "sub", -1)

    stride = 4 * cap + SUB
    send, slot = pl.pallas_call(
        functools.partial(splat_kernel, devices, cap),
        out_shape=(
            struct((devices * stride, LANES)),
            struct((blocks,), I32),
        ),
        in_specs=[vmem(), vmem(), vmem(), smem(), smem()],
        out_specs=(vmem(), smem()),
        scratch_shapes=[pltpu.SMEM((devices,), I32), pltpu.VMEM((8 * SUB, LANES), F32)],
        compiler_params=params(),
        name="splat",
    )(vel, weight, offset, owner[:, 0], brick[:, 0])

    exchange = functools.partial(
        lax.all_to_all, axis_name=("slab", "sub"), split_axis=0, concat_axis=0, tiled=True
    )
    arrived = exchange(send.reshape(devices, stride, LANES))
    arrived_brick = arrived[:, 4 * cap, :cap].astype(I32)
    count = jnp.sum((arrived_brick >= 0).astype(I32), axis=1)
    arrived_brick = arrived_brick.reshape(devices * cap)

    is_open = flags != 2
    next_x = jnp.concatenate([is_open[1:], wall_x > 0.0], 0)
    next_y = jnp.concatenate([is_open[:, 1:], wall_y > 0.0], 1)
    next_z = jnp.concatenate([is_open[:, :, 1:], jnp.zeros((span_x, span_y, 1), bool)], 2)
    code = (
        (is_open & next_x).astype(I32)
        + 2 * (is_open & next_y).astype(I32)
        + 4 * (is_open & next_z).astype(I32)
        + 8 * (flags == 1).astype(I32)
    ).reshape(grid4)

    whole = lambda *shape: pl.BlockSpec(shape, lambda x: (0,) * len(shape))
    one_layer = pl.BlockSpec((1, span_y, SUB, LANES), lambda x: (x, 0, 0, 0))
    three = pl.BlockSpec((3, 1, span_y, SUB, LANES), lambda x: (0, x, 0, 0, 0))
    g, r, div, edge_x, edge_y = pl.pallas_call(
        functools.partial(grid_kernel, devices, cap),
        grid=(span_x,),
        out_shape=(
            struct((3,) + grid4),
            struct((3,) + grid4),
            struct(grid4),
            struct((span_y, SUB, LANES)),
            struct((span_x, 1, SUB, LANES)),
        ),
        in_specs=[whole(devices * stride, LANES), smem(), smem(), one_layer],
        out_specs=(
            three,
            three,
            one_layer,
            whole(span_y, SUB, LANES),
            pl.BlockSpec((1, 1, SUB, LANES), lambda x: (x, 0, 0, 0)),
        ),
        scratch_shapes=[
            pltpu.VMEM((4, bricks, LANES), F32),
            pltpu.VMEM((span_y, SUB, LANES), F32),
            pltpu.VMEM((span_y + 1, SUB, LANES), F32),
        ],
        compiler_params=params(dimension_semantics=("arbitrary",)),
        name="grid",
    )(arrived.reshape(devices * stride, LANES), arrived_brick, count, code)

    padded = (span_x + 2, span_y + 2, SUB, LANES)
    p, reply = pl.pallas_call(
        functools.partial(solve_kernel, devices, cap),
        out_shape=(struct(padded), struct((devices * 3 * cap, LANES))),
        in_specs=[anywhere()] * 6 + [smem()],
        out_specs=(anywhere(), vmem()),
        scratch_shapes=[
            pltpu.VMEM((span_x + 1, span_y, SUB, LANES), F32),
            pltpu.VMEM((span_x, span_y + 1, SUB, LANES), F32),
            pltpu.VMEM(grid4, F32),
            pltpu.VMEM(grid4, F32),
            pltpu.VMEM(grid4, I32),
            pltpu.VMEM((3, bricks, LANES), F32),
            pltpu.VMEM((span_y, SUB, LANES), F32),
            pltpu.VMEM((span_x, SUB, LANES), F32),
            pltpu.VMEM(padded, F32),
            pltpu.VMEM(padded, F32),
            pltpu.VMEM(padded, F32),
            pltpu.SemaphoreType.DMA((6,)),
            pltpu.SemaphoreType.DMA,
            pltpu.SemaphoreType.DMA((16,)),
            pltpu.SemaphoreType.DMA((16,)),
        ],
        compiler_params=params(collective_id=0, has_side_effects=True),
        name="solve",
    )(g.reshape(3, bricks, LANES), r, div, code, edge_x, edge_y, arrived_brick)

    returned = exchange(reply.reshape(devices, 3 * cap, LANES))

    solved, pressure = pl.pallas_call(
        face_kernel,
        grid=(span_x,),
        out_shape=(struct((3,) + flags.shape), struct(flags.shape)),
        in_specs=[
            three,
            three,
            pl.BlockSpec((1, span_y + 2, SUB, LANES), lambda x: (x + 1, 0, 0, 0)),
            pl.BlockSpec((1, span_y + 2, SUB, LANES), lambda x: (x + 2, 0, 0, 0)),
        ],
        out_specs=(
            pl.BlockSpec((3, 1, span_y, span_z), lambda x: (0, x, 0, 0)),
            pl.BlockSpec((1, span_y, span_z), lambda x: (x, 0, 0)),
        ),
        scratch_shapes=[pltpu.VMEM((4, SUB * SUB, LANES), F32)],
        compiler_params=params(dimension_semantics=("arbitrary",)),
        cost_estimate=pl.CostEstimate(flops=10**7, bytes_accessed=24 * 10**6, transcendentals=0),
        name="faces",
    )(g, r, p, p)

    updated = pl.pallas_call(
        functools.partial(gather_kernel, cap),
        out_shape=struct((3, blocks, LANES)),
        in_specs=[vmem(), vmem(), smem(), vmem()],
        out_specs=vmem(),
        scratch_shapes=[pltpu.VMEM((3 * SUB, LANES), F32)],
        compiler_params=params(),
        name="gather",
    )(vel, offset, slot, returned.reshape(devices * 3 * cap, LANES))
    return updated.transpose(1, 0, 2), pressure, solved


def solution(mesh):
    in_specs = (
        P(("slab", "sub"), None, None),
        P(("slab", "sub"), None),
        P(("slab", "sub"), None),
        P(("slab", "sub"), None),
        P(("slab", "sub"), None),
        P("slab", "sub", None),
    )
    out_specs = (
        P(("slab", "sub"), None, None),
        P("slab", "sub", None),
        P(None, "slab", "sub", None),
    )
    return jax.shard_map(
        on_device, mesh=mesh, in_specs=in_specs, out_specs=out_specs, check_vma=False
    )
```
